128 devices in a mesh: dp: 4 (over z), expert: 32 (over x, y, core).
Axes of the slice: x: 4, y: 4, z: 4, core: 2. Of those that a mesh axis runs over, the one named last changes fastest.
Arguments:
- tokens: bfloat16 [4, 8192, 2048], P('dp', 'expert'), may hold values from -8 to 8
- cotangent: bfloat16 [4, 8192, 2048], P('dp', 'expert'), may hold values from -8 to 8
- slot_rows: int32 [4, 32, 32, 32], P('dp', 'expert'), may hold values from 0 to 255, as said below
- slot_count: int32 [4, 32, 32], P('dp', 'expert'), may hold values from 8 to 32, as said below
- slot_weight: float32 [4, 32, 32, 32], P('dp', 'expert'), may hold values from 0.1 to 1
- w_in: bfloat16 [32, 2, 2048, 512], P('expert'), may hold values from -5 to 5
- w_out: bfloat16 [32, 512, 2048], P('expert'), may hold values from -5 to 5
- momentum_in: float32 [32, 2, 2048, 512], P('expert', None, 'dp'), may hold values from -6 to 6
- momentum_out: float32 [32, 512, 2048], P('expert', None, 'dp'), may hold values from -6 to 6
Outputs:
- token_grad: bfloat16 [4, 8192, 2048], P('dp', 'expert')
- w_in_new: bfloat16 [32, 2, 2048, 512], P('expert')
- w_out_new: bfloat16 [32, 512, 2048], P('expert')
- momentum_in_new: float32 [32, 2, 2048, 512], P('expert', None, 'dp')
- momentum_out_new: float32 [32, 512, 2048], P('expert', None, 'dp')
The draws below stay inside these ranges and needn't reach their ends.
Inputs may be any that keep to these rules, and one draw needn't show every extreme that they name: `slot_rows`: entries index the source's 256 tokens; the 32 entries of one source and expert are distinct. Slots c < slot_count are used. In every replica some expert receives 32 rows from every source.
All inputs are finite; a program needn't handle non-finite values.
Results may differ from the reference program's by a relative error of at most 0.0064.
Values may be sent and summed in bfloat16 or wider, within the bound.
A program may use at most 128 MiB of HBM per device.

```python
import math
import jax
import jax.numpy as jnp
from jax import lax

D = 2048
FF = 512
LEVELS = 2
TOK_DEV = 256
CAP = 32
EXPERTS = 32
TOKENS = 8192
ROWS = 1024
N_DP = 4
N_EXPERT = 32


def feature_draw(key, rows_total, feature_width):
    key_scale = jax.random.fold_in(key, 0)
    key_common = jax.random.fold_in(key, 1)
    key_noise = jax.random.fold_in(key, 2)
    key_own = jax.random.fold_in(key, 4)
    key_replica = jax.random.fold_in(key, 5)
    column_scale = jnp.exp(jax.random.uniform(key_scale, (feature_width,), jnp.float32, 0.0, math.log(10.0)))
    column_scale = column_scale / jnp.sqrt(jnp.mean(column_scale * column_scale))
    shared = jax.random.normal(key_common, (1, 1, feature_width), jnp.float32)
    own = jax.random.normal(key_own, (N_DP, 1, feature_width), jnp.float32)
    replica_scale = jnp.exp(jax.random.uniform(key_replica, (N_DP, 1, 1), jnp.float32, math.log(0.6), math.log(1.6)))
    noise_part = jax.random.normal(key_noise, (N_DP, rows_total, feature_width), jnp.float32)
    result = replica_scale * (0.5 * (shared + 0.8 * own) + noise_part) * column_scale
    return jnp.clip(result, -8.0, 8.0)


def draw_tokens(key, part):
    return feature_draw(jax.random.fold_in(key, 11), TOKENS, D).astype(jnp.bfloat16)


def draw_cotangent(key, part):
    return feature_draw(jax.random.fold_in(key, 23), TOKENS, D).astype(jnp.bfloat16)


def draw_slot_rows(key, part):
    scores = jax.random.randint(jax.random.fold_in(key, 31), (N_DP, N_EXPERT, EXPERTS, TOK_DEV), 0, (1 << 30) // TOK_DEV)
    scores = scores * TOK_DEV + lax.broadcasted_iota(jnp.int32, scores.shape, 3)
    chosen = jnp.argsort(scores, axis=-1, stable=True)[..., :CAP]
    return chosen.astype(jnp.int32)


def draw_slot_count(key, part):
    key_counts, key_full = jax.random.split(jax.random.fold_in(key, 47))
    lowest = max(1, CAP // 4)
    counts = jax.random.randint(key_counts, (N_DP, N_EXPERT, EXPERTS), lowest, CAP + 1)
    full_expert = jax.random.randint(key_full, (N_DP, 1, 1), 0, EXPERTS)
    expert_ids = lax.broadcasted_iota(jnp.int32, counts.shape, 2)
    return jnp.where(expert_ids == full_expert, CAP, counts).astype(jnp.int32)


def shard_levels(rng, dims, cuts, smallest, top_value):
    level, own = 1.0, jax.random.fold_in(rng, 6)
    for axis_at, shards_of in cuts:
        draws = jnp.exp(jax.random.uniform(jax.random.fold_in(own, axis_at), (shards_of,), jnp.float32, smallest / len(cuts), top_value / len(cuts)))
        level = level * jnp.repeat(draws, dims[axis_at] // shards_of).reshape([-1 if axis == axis_at else 1 for axis in range(len(dims))])
    return level


def normal_values(rng, shape, width, most, cuts=(), kind=jnp.bfloat16):
    values = jax.random.normal(rng, shape, jnp.float32) * width
    if len(cuts) > 0:
        values = shard_levels(rng, shape, cuts, -0.22, 0.18) * values
    return jnp.clip(values, min=-most, max=most).astype(kind)


def setup_inputs(seed: int = 0) -> dict:
    key_of = jax.random.split(jax.random.key(seed), 10)
    tokens = draw_tokens(jax.random.fold_in(key_of[9], 71), 0)
    cotangent = draw_cotangent(jax.random.fold_in(key_of[9], 71), 0)
    slot_rows = draw_slot_rows(jax.random.fold_in(key_of[9], 71), 0)
    slot_count = draw_slot_count(jax.random.fold_in(key_of[9], 71), 0)
    slot_weight = jnp.clip(jnp.exp(math.log(1.0) - 2.3025851 * jax.random.uniform(key_of[4], (N_DP, N_EXPERT, EXPERTS, CAP), jnp.float32) ** shard_levels(key_of[4], (N_DP, N_EXPERT, EXPERTS, CAP), ((0, 4), (1, 32)), -0.2, 0.2)), 0.1, 1.0)
    w_in = normal_values(key_of[5], (EXPERTS, 2, D, FF), 1.0, 5.0, ((0, 32),))
    w_out = normal_values(key_of[6], (EXPERTS, FF, D), 1.0, 5.0, ((0, 32),))
    momentum_in = normal_values(key_of[7], (EXPERTS, 2, D, FF), 1.0, 6.0, ((0, 32), (2, 4)), jnp.float32)
    momentum_out = normal_values(key_of[8], (EXPERTS, FF, D), 1.0, 6.0, ((0, 32), (2, 4)), jnp.float32)
    return {"tokens": tokens, "cotangent": cotangent, "slot_rows": slot_rows, "slot_count": slot_count, "slot_weight": slot_weight, "w_in": w_in, "w_out": w_out, "momentum_in": momentum_in, "momentum_out": momentum_out}


adasum_eps = 1e-6
momentum_coef = 0.9
learn_rate = 0.1


def expert_backward(routed_rows, cotan_rows, w_gate, w_up, w_down):
    scale_in = routed_rows.shape[1] ** -0.5
    scale_out = w_gate.shape[1] ** -0.5
    gate_proj = jnp.dot(routed_rows, w_gate, preferred_element_type=jnp.float32) * scale_in
    up_proj = jnp.dot(routed_rows, w_up, preferred_element_type=jnp.float32) * scale_in
    sigmoid_gate = jax.nn.sigmoid(gate_proj)
    activated = gate_proj * sigmoid_gate
    hidden_act = (activated * up_proj).astype(jnp.bfloat16)
    grad_down = jnp.dot(hidden_act.T, cotan_rows, preferred_element_type=jnp.float32) * scale_out
    hidden_grad = jnp.dot(cotan_rows, w_down.T, preferred_element_type=jnp.float32) * scale_out
    gate_grad = (hidden_grad * up_proj * sigmoid_gate * (1.0 + gate_proj * (1.0 - sigmoid_gate))).astype(jnp.bfloat16)
    up_grad = (hidden_grad * activated).astype(jnp.bfloat16)
    grad_gate = jnp.dot(routed_rows.T, gate_grad, preferred_element_type=jnp.float32) * scale_in
    grad_up = jnp.dot(routed_rows.T, up_grad, preferred_element_type=jnp.float32) * scale_in
    rows_back = (jnp.dot(gate_grad, w_gate.T, preferred_element_type=jnp.float32)
                 + jnp.dot(up_grad, w_up.T, preferred_element_type=jnp.float32)) * scale_in
    return jnp.stack([grad_gate, grad_up]), grad_down, rows_back.astype(jnp.bfloat16)


def inner_terms(former, latter):
    return jnp.sum(former[0] * latter[0]) + jnp.sum(former[1] * latter[1])


def adasum(former, latter):
    cross_term = inner_terms(former, latter)
    coef_former = 1.0 - cross_term / (2.0 * (inner_terms(former, former) + adasum_eps))
    coef_latter = 1.0 - cross_term / (2.0 * (inner_terms(latter, latter) + adasum_eps))
    return (coef_former * former[0] + coef_latter * latter[0], coef_former * former[1] + coef_latter * latter[1])


def reference(tokens, cotangent, slot_rows, slot_count, slot_weight, w_in, w_out, momentum_in, momentum_out):
    is_valid = (jnp.arange(CAP, dtype=jnp.int32)[None, None, None, :] < slot_count[:, :, :, None]).astype(jnp.float32)
    slot_scale = slot_weight * is_valid
    offsets = (jnp.arange(N_EXPERT, dtype=jnp.int32) * TOK_DEV)[None, :, None, None]
    token_index = (slot_rows + offsets).astype(jnp.int32)

    def per_expert(token_grad, expert_id):
        chosen = lax.dynamic_index_in_dim(token_index, expert_id, 2, keepdims=False).reshape(N_DP, ROWS)
        scales = lax.dynamic_index_in_dim(slot_scale, expert_id, 2, keepdims=False).reshape(N_DP, ROWS)
        w_pair = lax.dynamic_index_in_dim(w_in, expert_id, 0, keepdims=False)
        w_down = lax.dynamic_index_in_dim(w_out, expert_id, 0, keepdims=False)
        vectors = []
        for replica in range(N_DP):
            routed_rows = tokens[replica][chosen[replica]]
            cotan_rows = (cotangent[replica][chosen[replica]].astype(jnp.float32) * scales[replica][:, None]).astype(jnp.bfloat16)
            grad_wide, grad_narrow, rows_back = expert_backward(routed_rows, cotan_rows, w_pair[0], w_pair[1], w_down)
            token_grad = token_grad.at[replica, chosen[replica]].add(rows_back.astype(jnp.float32))
            vectors.append((grad_wide, grad_narrow))
        for level_bit in range(LEVELS - 1, -1, -1):
            stride = 2 ** level_bit
            vectors = [adasum(vectors[lower_id], vectors[lower_id + stride]) for lower_id in range(stride)]
        combined = vectors[0]
        momentum_wide = momentum_coef * lax.dynamic_index_in_dim(momentum_in, expert_id, 0, keepdims=False) + combined[0]
        momentum_narrow = momentum_coef * lax.dynamic_index_in_dim(momentum_out, expert_id, 0, keepdims=False) + combined[1]
        new_wide = (w_pair.astype(jnp.float32) - learn_rate * momentum_wide).astype(jnp.bfloat16)
        new_narrow = (w_down.astype(jnp.float32) - learn_rate * momentum_narrow).astype(jnp.bfloat16)
        return token_grad, (new_wide, new_narrow, momentum_wide, momentum_narrow)

    initial = jnp.zeros((N_DP, TOKENS, D), jnp.float32)
    token_grad, stacked = lax.scan(per_expert, initial, jnp.arange(EXPERTS, dtype=jnp.int32))
    return (token_grad.astype(jnp.bfloat16), stacked[0], stacked[1], stacked[2], stacked[3])
```

```python
import jax
import jax.numpy as jnp
from jax import lax
from jax.experimental import pallas as pl
from jax.experimental.pallas import tpu as pltpu
from jax.sharding import PartitionSpec as P

EPS = 1e-06
MOMENTUM = 0.9
RATE = 0.1
MESH = pl.DeviceIdType.MESH

D = 2048
FF = 512
HALF = 1024
QUARTER = 512
CAP = 32
STAGES_X = 2
STAGES_G = 4
STAGES_R = 2
ROWS = 1024
BF16 = jnp.bfloat16
F32 = jnp.float32


def dot(a, b, ca, cb):
    return lax.dot_general(a, b, (((ca,), (cb,)), ((), ())), preferred_element_type=F32)


def kernel(
    tok_h, cot_h, rows_v, count_v, weight_v, win_h, wout_h, min_h, mout_h,
    tg_h, nwin_h, nwout_h, nmin_h, nmout_h,
    tok, cot, onehot, scale, send_x, send_g, mid_x, mid_g, xs, gs_, win, wout,
    act_a, act_s, hid, dh, dgu, grad_s, grad_r, mom_in, mom_out, gram,
    load_sem, p1_send, p1_recv, p2_send, p2_recv, self1, self2,
    rs_send, rs_recv, rs_self, gram_send, gram_recv, ag_send, ag_recv, fw_send, fw_recv, out_sem,
):
    z = lax.axis_index("dp")
    e = lax.axis_index("expert")
    x = e // 8
    y = lax.rem(e // 2, 4)
    c = lax.rem(e, 2)
    scale_in = D ** (-0.5)
    scale_out = FF ** (-0.5)

    def expert_id(px, py, pc):
        return (px * 4 + py) * 2 + pc

    loads = [
        (tok_h, tok), (cot_h, cot), (win_h, win), (wout_h, wout), (min_h, mom_in), (mout_h, mom_out),
    ]
    load = [pltpu.make_async_copy(s, d, load_sem.at[i]) for i, (s, d) in enumerate(loads)]
    for copy in load:
        copy.start()

    barrier = pltpu.get_barrier_semaphore()

    def greet(device):
        pl.semaphore_signal(barrier, inc=1, device_id=device, device_id_type=MESH)

    for k in range(1, 8):
        greet((z, expert_id(lax.rem(x + k // 2, 4), y, lax.rem(c + k % 2, 2))))
    for k in range(2, 8):
        greet((z, expert_id(x, lax.rem(y + k // 2, 4), lax.rem(c + k % 2, 2))))
    for k in range(1, 4):
        greet((lax.rem(z + k, 4), e))

    rows_t = rows_v[...]
    weight_t = weight_v[...]
    valid = lax.broadcasted_iota(jnp.int32, (CAP, 32), 0) < count_v[...]
    scale_t = jnp.where(valid, weight_t, 0.0)
    lane = lax.broadcasted_iota(jnp.int32, (CAP, 256), 1)
    for k in range(32):
        onehot[k * CAP : (k + 1) * CAP, :] = (lane == rows_t[:, k : k + 1]).astype(F32).astype(BF16)
        scale[k * CAP : (k + 1) * CAP, :] = jnp.broadcast_to(scale_t[:, k : k + 1], (CAP, 128))

    def gather(src, dst, c0, w, scaled):
        def step(m, _):
            r0 = pl.multiple_of(m * 256, 256)
            hot = onehot[pl.ds(r0, 256), :]
            for half in range(2):
                col = half * HALF + c0
                v = dot(hot, src[:, col : col + w], 1, 0)
                if scaled:
                    v = v * scale[pl.ds(r0, 256), 0:1]
                dst[m, :, :, :, col : col + w] = v.astype(BF16).reshape(4, 2, CAP, w)
            return 0

        lax.fori_loop(0, 4, step, 0)

    def p1_copy(send, mid, st, c0, w, half, k):
        pc = lax.rem(c + lax.rem(k, 2), 2)
        col = pl.ds(half * HALF + c0, w)
        mcol = pl.ds(c0, w)
        if half == 0:
            pa = lax.rem(x + k // 2, 4)
            peer = expert_id(pa, y, pc)
            src = send.at[pa, :, pc, :, col]
            dst = mid.at[0, :, x, c, :, mcol]
        else:
            pa = lax.rem(y + k // 2, 4)
            peer = expert_id(x, pa, pc)
            src = send.at[:, pa, pc, :, col]
            dst = mid.at[1, :, y, c, :, mcol]
        return pltpu.make_async_remote_copy(
            src_ref=src, dst_ref=dst, send_sem=p1_send.at[st, half, k], recv_sem=p1_recv.at[st, half, k],
            device_id=(z, peer), device_id_type=MESH,
        )

    def p1_self(send, mid, st, c0, w, half):
        col = pl.ds(half * HALF + c0, w)
        mcol = pl.ds(c0, w)
        if half == 0:
            return pltpu.make_async_copy(
                send.at[x, :, c, :, col], mid.at[0, :, x, c, :, mcol], self1.at[st, half]
            )
        return pltpu.make_async_copy(
            send.at[:, y, c, :, col], mid.at[1, :, y, c, :, mcol], self1.at[st, half]
        )

    def p2_copy(mid, fin, st, c0, w, half, k):
        col = pl.ds(half * HALF + c0, w)
        mcol = pl.ds(c0, w)
        if half == 0:
            pa = lax.rem(y + k, 4)
            peer = expert_id(x, pa, c)
            src = mid.at[0, pa, :, :, :, mcol]
            dst = fin.at[:, y, :, :, col]
        else:
            pa = lax.rem(x + k, 4)
            peer = expert_id(pa, y, c)
            src = mid.at[1, pa, :, :, :, mcol]
            dst = fin.at[x, :, :, :, col]
        return pltpu.make_async_remote_copy(
            src_ref=src, dst_ref=dst, send_sem=p2_send.at[st, half, k], recv_sem=p2_recv.at[st, half, k],
            device_id=(z, peer), device_id_type=MESH,
        )

    def p2_self(mid, fin, st, c0, w, half):
        col = pl.ds(half * HALF + c0, w)
        mcol = pl.ds(c0, w)
        if half == 0:
            return pltpu.make_async_copy(
                mid.at[0, y, :, :, :, mcol], fin.at[:, y, :, :, col], self2.at[st, half]
            )
        return pltpu.make_async_copy(
            mid.at[1, x, :, :, :, mcol], fin.at[x, :, :, :, col], self2.at[st, half]
        )

    def each(lo, hi, fn):
        def step(k, _):
            fn(k)
            return 0

        lax.fori_loop(lo, hi, step, 0)

    def start_first(args):
        send, mid, fin, st, c0, w = args

        def go(k):
            p1_copy(send, mid, st, c0, w, 0, k).start()
            p1_copy(send, mid, st, c0, w, 1, k).start()

        each(1, 8, go)
        for half in range(2):
            p1_self(send, mid, st, c0, w, half).start()

    def forward(args):
        send, mid, fin, st, c0, w = args
        for half in range(2):
            each(1, 8, lambda k: p1_copy(send, mid, st, c0, w, half, k).wait())
            p1_self(send, mid, st, c0, w, half).wait()
            each(1, 4, lambda k: p2_copy(mid, fin, st, c0, w, half, k).start())
            p2_self(mid, fin, st, c0, w, half).start()

    def arrive(args):
        send, mid, fin, st, c0, w = args
        for half in range(2):
            each(1, 4, lambda k: p2_copy(mid, fin, st, c0, w, half, k).wait())
            p2_self(mid, fin, st, c0, w, half).wait()

    wx, wg, wr = HALF // STAGES_X, HALF // STAGES_G, HALF // STAGES_R
    ex = [(send_x, mid_x, xs, s, s * wx, wx) for s in range(STAGES_X)]
    eg = [(send_g, mid_g, gs_, STAGES_X + s, s * wg, wg) for s in range(STAGES_G)]
    er = [(send_x, mid_x, send_g, STAGES_X + STAGES_G + s, s * wr, wr) for s in range(STAGES_R)]

    def activate(m):
        rows = xs[m].reshape(256, D)
        r = pl.ds(pl.multiple_of(m * 256, 256), 256)
        gate = dot(rows, win[0], 1, 0) * scale_in
        up = dot(rows, win[1], 1, 0) * scale_in
        sig = jax.nn.sigmoid(gate)
        act = gate * sig
        hid[r, :] = (act * up).astype(BF16)
        act_a[r, :] = up * sig * (1.0 + gate * (1.0 - sig))
        act_s[r, :] = act

    def out_copy(s, half):
        col = half * HALF + s * wg
        q, off = col // QUARTER, col % QUARTER
        return q, pltpu.make_async_remote_copy(
            src_ref=grad_s.at[2, q, :, pl.ds(off, wg)],
            dst_ref=grad_r.at[z, 2, :, pl.ds(off, wg)],
            send_sem=rs_send.at[2, s, half],
            recv_sem=rs_recv.at[2 + off // wg, lax.rem(q - z + 4, 4)],
            device_id=(q, e), device_id_type=MESH,
        ), pltpu.make_async_copy(
            grad_s.at[2, q, :, pl.ds(off, wg)], grad_r.at[z, 2, :, pl.ds(off, wg)], rs_self.at[2, s, half]
        )

    def grad_out(s):
        for half in range(2):
            col = half * HALF + s * wg
            q, off = col // QUARTER, col % QUARTER
            rows = gs_[:, :, :, :, col : col + wg].reshape(ROWS, wg)
            grad_s[2, q, :, off : off + wg] = (dot(hid[...], rows, 0, 0) * scale_out).astype(BF16)
            q, remote, local = out_copy(s, half)

            @pl.when(z != q)
            def _():
                remote.start()

            @pl.when(z == q)
            def _():
                local.start()

    def hidden_grad(s):
        def step(m, _):
            r = pl.ds(pl.multiple_of(m * 256, 256), 256)
            acc = None
            for half in range(2):
                col = half * HALF + s * wg
                rows = gs_[m, :, :, :, col : col + wg].reshape(256, wg)
                part = dot(rows, wout[:, col : col + wg], 1, 1)
                acc = part if acc is None else acc + part
            if s > 0:
                acc = acc + dh[r, :]
            if s < STAGES_G - 1:
                dh[r, :] = acc
            else:
                acc = acc * scale_out
                dgu[0, r, :] = (acc * act_a[r, :]).astype(BF16)
                dgu[1, r, :] = (acc * act_s[r, :]).astype(BF16)
            return 0

        lax.fori_loop(0, 4, step, 0)

    def in_copy(mat, k):
        q = lax.rem(z + k, 4)
        return pltpu.make_async_remote_copy(
            src_ref=grad_s.at[mat, q], dst_ref=grad_r.at[z, mat],
            send_sem=rs_send.at[mat, k, 0], recv_sem=rs_recv.at[mat, k],
            device_id=(q, e), device_id_type=MESH,
        )

    def in_self(mat):
        return pltpu.make_async_copy(grad_s.at[mat, z], grad_r.at[z, mat], rs_self.at[mat, 0, 0])

    def grad_in(mat):
        def step(j, _):
            k = lax.rem(2 + 3 * j, 4)
            q = lax.rem(z + k, 4)
            rows = xs[:, :, :, :, pl.ds(pl.multiple_of(q * QUARTER, QUARTER), QUARTER)].reshape(ROWS, QUARTER)
            grad_s[mat, q] = (dot(rows, dgu[mat], 0, 0) * scale_in).astype(BF16)

            @pl.when(k != 0)
            def _():
                in_copy(mat, k).start()

            @pl.when(k == 0)
            def _():
                in_self(mat).start()

            return 0

        lax.fori_loop(0, 4, step, 0)

    def rows_back(s):
        def step(m, _):
            r = pl.ds(pl.multiple_of(m * 256, 256), 256)
            for half in range(2):
                col = half * HALF + s * wr
                v = dot(dgu[0, r, :], win[0, col : col + wr, :], 1, 1)
                v = v + dot(dgu[1, r, :], win[1, col : col + wr, :], 1, 1)
                send_x[m, :, :, :, col : col + wr] = (v * scale_in).astype(BF16).reshape(4, 2, CAP, wr)
            return 0

        lax.fori_loop(0, 4, step, 0)

    pairs = [(0, 0), (1, 1), (2, 2), (3, 3), (0, 1), (0, 2), (0, 3), (1, 2), (1, 3), (2, 3)]

    def fold(v):
        total = None
        for i in range(v.shape[0] // 8):
            for j in range(v.shape[1] // 128):
                part = v[i * 8 : (i + 1) * 8, j * 128 : (j + 1) * 128]
                total = part if total is None else total + part
        return total

    def gram_of(mat, sums):
        def step(i, sums):
            r = pl.ds(pl.multiple_of(i * 16, 16), 16)
            g = [grad_r[s, mat, r, :].astype(F32) for s in range(4)]
            return tuple(t + fold(g[a] * g[b]) for t, (a, b) in zip(sums, pairs))

        return lax.fori_loop(0, 32, step, sums)

    load[0].wait()
    gather(tok, send_x, ex[0][4], wx, False)
    pl.semaphore_wait(barrier, 16)
    start_first(ex[0])
    gather(tok, send_x, ex[1][4], wx, False)
    start_first(ex[1])
    load[1].wait()
    gather(cot, send_g, eg[0][4], wg, True)
    gather(cot, send_g, eg[1][4], wg, True)
    forward(ex[0])
    start_first(eg[0])
    gather(cot, send_g, eg[2][4], wg, True)
    gather(cot, send_g, eg[3][4], wg, True)
    forward(ex[1])
    start_first(eg[1])
    forward(eg[0])
    start_first(eg[2])
    load[2].wait()
    load[3].wait()
    arrive(ex[0])
    arrive(ex[1])
    start_first(eg[3])
    each(0, 2, activate)
    forward(eg[1])
    each(2, 4, activate)
    forward(eg[2])
    arrive(eg[0])
    grad_out(0)
    hidden_grad(0)
    arrive(eg[1])
    grad_out(1)
    hidden_grad(1)
    forward(eg[3])
    arrive(eg[2])
    grad_out(2)
    hidden_grad(2)
    arrive(eg[3])
    grad_out(3)
    hidden_grad(3)
    grad_in(0)
    grad_in(1)
    for s in range(STAGES_R):
        rows_back(s)
        start_first(er[s])

    sums = tuple(jnp.zeros((8, 128), F32) for _ in pairs)
    for k in range(1, 4):
        for j in range(QUARTER // wg):
            pltpu.make_async_remote_copy(
                src_ref=grad_s.at[2, 0, :, pl.ds(j * wg, wg)],
                dst_ref=grad_r.at[lax.rem(z - k + 4, 4), 2, :, pl.ds(j * wg, wg)],
                send_sem=rs_send.at[2, 0, 0], recv_sem=rs_recv.at[2 + j, k],
                device_id=(lax.rem(z + k, 4), e), device_id_type=MESH,
            ).wait_recv()
    for s in range(STAGES_G):
        for half in range(2):
            q, remote, local = out_copy(s, half)

            @pl.when(z != q)
            def _():
                remote.wait_send()

            @pl.when(z == q)
            def _():
                local.wait()

    sums = gram_of(2, sums)
    for s in range(STAGES_R):
        forward(er[s])
    for mat in range(2):
        each(1, 4, lambda k: in_copy(mat, k).wait())
        in_self(mat).wait()
        sums = gram_of(mat, sums)

    own = jnp.concatenate([jnp.sum(t, axis=0, keepdims=True) for t in sums] + [jnp.zeros((6, 128), F32)], axis=0)
    gram[z] = own

    def gram_copy(k):
        return pltpu.make_async_remote_copy(
            src_ref=gram.at[z], dst_ref=gram.at[z], send_sem=gram_send.at[k], recv_sem=gram_recv.at[k],
            device_id=(lax.rem(z + k, 4), e), device_id_type=MESH,
        )

    each(1, 4, lambda k: gram_copy(k).start())
    load[4].wait()
    load[5].wait()
    each(1, 4, lambda k: gram_copy(k).wait())
    total = jnp.sum(gram[0] + gram[1] + gram[2] + gram[3], axis=1, keepdims=True)
    dots = {p: total[i : i + 1, :] for i, p in enumerate(pairs)}

    def coefficient(cross, norm):
        return 1.0 - cross / (2.0 * (norm + EPS))

    a0 = coefficient(dots[0, 2], dots[0, 0])
    a2 = coefficient(dots[0, 2], dots[2, 2])
    a1 = coefficient(dots[1, 3], dots[1, 1])
    a3 = coefficient(dots[1, 3], dots[3, 3])
    n0 = a0 * a0 * dots[0, 0] + 2.0 * a0 * a2 * dots[0, 2] + a2 * a2 * dots[2, 2]
    n1 = a1 * a1 * dots[1, 1] + 2.0 * a1 * a3 * dots[1, 3] + a3 * a3 * dots[3, 3]
    cross = a0 * (a1 * dots[0, 1] + a3 * dots[0, 3]) + a2 * (a1 * dots[1, 2] + a3 * dots[2, 3])
    b0 = coefficient(cross, jnp.maximum(n0, 0.0))
    b1 = coefficient(cross, jnp.maximum(n1, 0.0))
    coef = [b0 * a0, b1 * a1, b0 * a2, b1 * a3]

    def slot(mat, hh, owner):
        if mat < 2:
            return nwin_h.at[mat, pl.ds(owner * QUARTER + hh * 256, 256), :]
        return nwout_h.at[pl.ds(hh * 256, 256), pl.ds(pl.multiple_of(owner * QUARTER, QUARTER), QUARTER)]

    def ag_copy(mat, hh, direction):
        return pltpu.make_async_remote_copy(
            src_ref=grad_s.at[mat, 0, pl.ds(hh * 256, 256), :], dst_ref=slot(mat, hh, z),
            send_sem=ag_send.at[direction, 2 * mat + hh], recv_sem=ag_recv.at[direction, 2 * mat + hh],
            device_id=(lax.rem(z + (1 if direction == 0 else 3), 4), e), device_id_type=MESH,
        )

    def fw_copy(mat, hh):
        owner = lax.rem(z + (3 if hh == 0 else 1), 4)
        return pltpu.make_async_remote_copy(
            src_ref=slot(mat, hh, owner), dst_ref=slot(mat, hh, owner),
            send_sem=fw_send.at[2 * mat + hh], recv_sem=fw_recv.at[2 * mat + hh],
            device_id=(lax.rem(z + (1 if hh == 0 else 3), 4), e), device_id_type=MESH,
        )

    def out_local(mat, hh):
        own_w = pltpu.make_async_copy(
            grad_s.at[mat, 0, pl.ds(hh * 256, 256), :], slot(mat, hh, z), out_sem.at[0, 2 * mat + hh]
        )
        if mat < 2:
            own_m = pltpu.make_async_copy(
                mom_in.at[mat, pl.ds(hh * 256, 256), :], nmin_h.at[mat, pl.ds(hh * 256, 256), :],
                out_sem.at[1, 2 * mat + hh],
            )
        else:
            own_m = pltpu.make_async_copy(
                mom_out.at[pl.ds(hh * 256, 256), :], nmout_h.at[pl.ds(hh * 256, 256), :],
                out_sem.at[1, 2 * mat + hh],
            )
        return own_w, own_m

    for mat in range(3):
        for hh in range(2):

            def step(i, _):
                r = pl.multiple_of(hh * 256 + i * 32, 32)
                rr = pl.ds(r, 32)
                comb = coef[0] * grad_r[0, mat, rr, :].astype(F32)
                for s in range(1, 4):
                    comb = comb + coef[s] * grad_r[s, mat, rr, :].astype(F32)
                if mat < 2:
                    new = MOMENTUM * mom_in[mat, rr, :] + comb
                    mom_in[mat, rr, :] = new
                    old = win[mat, pl.ds(pl.multiple_of(z * QUARTER + r, 32), 32), :]
                else:
                    new = MOMENTUM * mom_out[rr, :] + comb
                    mom_out[rr, :] = new
                    old = wout[rr, pl.ds(pl.multiple_of(z * QUARTER, QUARTER), QUARTER)]
                grad_s[mat, 0, rr, :] = (old.astype(F32) - RATE * new).astype(BF16)
                return 0

            lax.fori_loop(0, 8, step, 0)
            ag_copy(mat, hh, 0).start()
            ag_copy(mat, hh, 1).start()
            for copy in out_local(mat, hh):
                copy.start()

    def pass_on(mat, hh):
        ag_copy(mat, hh, hh).wait_recv()
        fw_copy(mat, hh).start()

    pass_on(0, 0)
    pass_on(0, 1)

    for s in range(STAGES_R):
        arrive(er[s])

    def tokens_step(n, _):
        cols = pl.ds(pl.multiple_of(n * 512, 512), 512)
        rows = send_g[:, :, :, :, cols].reshape(ROWS, 512)
        tok[:, cols] = dot(onehot[...], rows, 0, 0).astype(BF16)
        return 0

    lax.fori_loop(0, 4, tokens_step, 0)
    tok_out = pltpu.make_async_copy(tok, tg_h, load_sem.at[0])
    tok_out.start()

    for mat in range(1, 3):
        for hh in range(2):
            pass_on(mat, hh)
    for mat in range(3):
        for hh in range(2):
            ag_copy(mat, hh, 1 - hh).wait_recv()
            ag_copy(mat, hh, 0).wait_send()
            ag_copy(mat, hh, 1).wait_send()
            fw_copy(mat, hh).wait()
            for copy in out_local(mat, hh):
                copy.wait()
    tok_out.wait()


def shards(tokens, cotangent, slot_rows, slot_count, slot_weight, w_in, w_out, momentum_in, momentum_out):
    any_ = pl.BlockSpec(memory_space=pl.ANY)
    vmem = pl.BlockSpec(memory_space=pltpu.VMEM)
    stages = STAGES_X + STAGES_G + STAGES_R
    grid5 = (4, 4, 2, CAP, D)
    mid = (2, 4, 4, 2, CAP, HALF)
    dma = pltpu.SemaphoreType.DMA
    outs = pl.pallas_call(
        kernel,
        out_shape=(
            jax.ShapeDtypeStruct((256, D), BF16),
            jax.ShapeDtypeStruct((2, D, FF), BF16),
            jax.ShapeDtypeStruct((FF, D), BF16),
            jax.ShapeDtypeStruct((2, QUARTER, FF), F32),
            jax.ShapeDtypeStruct((FF, QUARTER), F32),
        ),
        in_specs=[any_, any_, vmem, vmem, vmem, any_, any_, any_, any_],
        out_specs=(any_, any_, any_, any_, any_),
        scratch_shapes=[
            pltpu.VMEM((256, D), BF16),
            pltpu.VMEM((256, D), BF16),
            pltpu.VMEM((ROWS, 256), BF16),
            pltpu.VMEM((ROWS, 128), F32),
            pltpu.VMEM(grid5, BF16),
            pltpu.VMEM(grid5, BF16),
            pltpu.VMEM(mid, BF16),
            pltpu.VMEM(mid, BF16),
            pltpu.VMEM(grid5, BF16),
            pltpu.VMEM(grid5, BF16),
            pltpu.VMEM((2, D, FF), BF16),
            pltpu.VMEM((FF, D), BF16),
            pltpu.VMEM((ROWS, FF), F32),
            pltpu.VMEM((ROWS, FF), F32),
            pltpu.VMEM((ROWS, FF), BF16),
            pltpu.VMEM((ROWS, FF), F32),
            pltpu.VMEM((2, ROWS, FF), BF16),
            pltpu.VMEM((3, 4, QUARTER, QUARTER), BF16),
            pltpu.VMEM((4, 3, QUARTER, QUARTER), BF16),
            pltpu.VMEM((2, QUARTER, FF), F32),
            pltpu.VMEM((FF, QUARTER), F32),
            pltpu.VMEM((4, 16, 128), F32),
            dma((6,)),
            dma((stages, 2, 8)),
            dma((stages, 2, 8)),
            dma((stages, 2, 4)),
            dma((stages, 2, 4)),
            dma((stages, 2)),
            dma((stages, 2)),
            dma((3, STAGES_G, 2)),
            dma((4, 4)),
            dma((3, STAGES_G, 2)),
            dma((4,)),
            dma((4,)),
            dma((2, 6)),
            dma((2, 6)),
            dma((6,)),
            dma((6,)),
            dma((2, 6)),
        ],
        compiler_params=pltpu.CompilerParams(
            collective_id=0, has_side_effects=True, vmem_limit_bytes=62 << 20
        ),
        name="step",
    )(
        tokens[0], cotangent[0], slot_rows[0, 0].T, slot_count[0], slot_weight[0, 0].T,
        w_in[0], w_out[0], momentum_in[0], momentum_out[0],
    )
    return tuple(o[None] for o in outs)


def solution(mesh):
    return jax.shard_map(
        shards,
        mesh=mesh,
        in_specs=(
            P("dp", "expert", None),
            P("dp", "expert", None),
            P("dp", "expert", None, None),
            P("dp", "expert", None),
            P("dp", "expert", None, None),
            P("expert", None, None, None),
            P("expert", None, None),
            P("expert", None, "dp", None),
            P("expert", None, "dp"),
        ),
        out_specs=(
            P("dp", "expert", None),
            P("expert", None, None, None),
            P("expert", None, None),
            P("expert", None, "dp", None),
            P("expert", None, "dp"),
        ),
        check_vma=False,
    )
```

```python
import jax
import jax.numpy as jnp
from jax import lax
from jax.experimental import pallas as pl
from jax.experimental.pallas import tpu as pltpu
from jax.sharding import PartitionSpec as P

EPS = 1e-06
MOMENTUM = 0.9
RATE = 0.1
MESH = pl.DeviceIdType.MESH

D = 2048
FF = 512
HALF = 1024
QUARTER = 512
CAP = 32
STAGES_X = 2
STAGES_G = 4
STAGES_R = 2
ROWS = 1024
ORDER_G = (0, 512, 256, 768)
BF16 = jnp.bfloat16
F32 = jnp.float32


def dot(a, b, ca, cb):
    return lax.dot_general(a, b, (((ca,), (cb,)), ((), ())), preferred_element_type=F32)


def kernel(
    tok_h, cot_h, rows_v, count_v, weight_v, win_h, wout_h, min_h, mout_h,
    tok, xs, nwout, mom_in, mom_out,
    cot, onehot, scale, send_x, send_g, mid_x, mid_g, gs_, win, wout,
    act_a, act_s, hid, dh, dgu, grad_s, grad_r, gram,
    load_sem, p1_send, p1_recv, p2_send, p2_recv, self1, self2,
    rs_send, rs_recv, rs_self, gram_send, gram_recv, ag_send, ag_recv, fw_send, fw_recv,
):
    z = lax.axis_index("dp")
    e = lax.axis_index("expert")
    x = e // 8
    y = lax.rem(e // 2, 4)
    c = lax.rem(e, 2)
    scale_in = D ** (-0.5)
    scale_out = FF ** (-0.5)

    def expert_id(px, py, pc):
        return (px * 4 + py) * 2 + pc

    loads = [
        (tok_h, tok), (cot_h, cot), (win_h, win), (wout_h, wout), (min_h, mom_in), (mout_h, mom_out),
    ]
    load = [pltpu.make_async_copy(s, d, load_sem.at[i]) for i, (s, d) in enumerate(loads)]
    for copy in load[:2]:
        copy.start()

    barrier = pltpu.get_barrier_semaphore()

    def greet(device):
        pl.semaphore_signal(barrier, inc=1, device_id=device, device_id_type=MESH)

    for k in range(1, 8):
        greet((z, expert_id(lax.rem(x + k // 2, 4), y, lax.rem(c + k % 2, 2))))
    for k in range(2, 8):
        greet((z, expert_id(x, lax.rem(y + k // 2, 4), lax.rem(c + k % 2, 2))))
    for k in range(1, 4):
        greet((lax.rem(z + k, 4), e))

    rows_t = jnp.transpose(rows_v[...])
    weight_t = jnp.transpose(weight_v[...])
    valid = lax.broadcasted_iota(jnp.int32, (CAP, 32), 0) < count_v[...]
    scale_t = jnp.where(valid, weight_t, 0.0)
    lane = lax.broadcasted_iota(jnp.int32, (CAP, 256), 1)
    for k in range(32):
        onehot[k * CAP : (k + 1) * CAP, :] = (lane == rows_t[:, k : k + 1]).astype(F32).astype(BF16)
        scale[k * CAP : (k + 1) * CAP, :] = jnp.broadcast_to(scale_t[:, k : k + 1], (CAP, 128))

    def gather(src, dst, c0, w, scaled):
        def step(m, _):
            r0 = pl.multiple_of(m * 256, 256)
            hot = onehot[pl.ds(r0, 256), :]
            for half in range(2):
                col = half * HALF + c0
                v = dot(hot, src[:, col : col + w], 1, 0)
                if scaled:
                    v = v * scale[pl.ds(r0, 256), 0:1]
                dst[m, :, :, :, col : col + w] = v.astype(BF16).reshape(4, 2, CAP, w)
            return 0

        lax.fori_loop(0, 4, step, 0)

    def p1_copy(send, mid, st, c0, w, half, k):
        pc = lax.rem(c + lax.rem(k, 2), 2)
        col = pl.ds(half * HALF + c0, w)
        mcol = pl.ds(c0, w)
        if half == 0:
            pa = lax.rem(x + k // 2, 4)
            peer = expert_id(pa, y, pc)
            src = send.at[pa, :, pc, :, col]
            dst = mid.at[0, :, x, c, :, mcol]
        else:
            pa = lax.rem(y + k // 2, 4)
            peer = expert_id(x, pa, pc)
            src = send.at[:, pa, pc, :, col]
            dst = mid.at[1, :, y, c, :, mcol]
        return pltpu.make_async_remote_copy(
            src_ref=src, dst_ref=dst, send_sem=p1_send.at[st, half, k], recv_sem=p1_recv.at[st, half, k],
            device_id=(z, peer), device_id_type=MESH,
        )

    def p1_self(send, mid, st, c0, w, half):
        col = pl.ds(half * HALF + c0, w)
        mcol = pl.ds(c0, w)
        if half == 0:
            return pltpu.make_async_copy(
                send.at[x, :, c, :, col], mid.at[0, :, x, c, :, mcol], self1.at[st, half]
            )
        return pltpu.make_async_copy(
            send.at[:, y, c, :, col], mid.at[1, :, y, c, :, mcol], self1.at[st, half]
        )

    def p2_copy(mid, fin, st, c0, w, half, k):
        col = pl.ds(half * HALF + c0, w)
        mcol = pl.ds(c0, w)
        if half == 0:
            pa = lax.rem(y + k, 4)
            peer = expert_id(x, pa, c)
            src = mid.at[0, pa, :, :, :, mcol]
            dst = fin.at[:, y, :, :, col] if fin is not xs else fin.at[c0 // QUARTER, :, y]
        else:
            pa = lax.rem(x + k, 4)
            peer = expert_id(pa, y, c)
            src = mid.at[1, pa, :, :, :, mcol]
            dst = fin.at[x, :, :, :, col] if fin is not xs else fin.at[2 + c0 // QUARTER, x]
        return pltpu.make_async_remote_copy(
            src_ref=src, dst_ref=dst, send_sem=p2_send.at[st, half, k], recv_sem=p2_recv.at[st, half, k],
            device_id=(z, peer), device_id_type=MESH,
        )

    def p2_self(mid, fin, st, c0, w, half):
        col = pl.ds(half * HALF + c0, w)
        mcol = pl.ds(c0, w)
        if half == 0:
            dst = fin.at[:, y, :, :, col] if fin is not xs else fin.at[c0 // QUARTER, :, y]
            return pltpu.make_async_copy(mid.at[0, y, :, :, :, mcol], dst, self2.at[st, half])
        dst = fin.at[x, :, :, :, col] if fin is not xs else fin.at[2 + c0 // QUARTER, x]
        return pltpu.make_async_copy(mid.at[1, x, :, :, :, mcol], dst, self2.at[st, half])

    def each(lo, hi, fn):
        def step(k, _):
            fn(k)
            return 0

        lax.fori_loop(lo, hi, step, 0)

    def start_first(args):
        send, mid, fin, st, c0, w = args

        def go(k):
            p1_copy(send, mid, st, c0, w, 0, k).start()
            p1_copy(send, mid, st, c0, w, 1, k).start()

        each(1, 8, go)
        for half in range(2):
            p1_self(send, mid, st, c0, w, half).start()

    def forward(args):
        send, mid, fin, st, c0, w = args
        for half in range(2):
            each(1, 8, lambda k: p1_copy(send, mid, st, c0, w, half, k).wait())
            p1_self(send, mid, st, c0, w, half).wait()
            each(1, 4, lambda k: p2_copy(mid, fin, st, c0, w, half, k).start())
            p2_self(mid, fin, st, c0, w, half).start()

    def arrive(args):
        send, mid, fin, st, c0, w = args
        for half in range(2):
            each(1, 4, lambda k: p2_copy(mid, fin, st, c0, w, half, k).wait())
            p2_self(mid, fin, st, c0, w, half).wait()

    wx, wg, wr = HALF // STAGES_X, HALF // STAGES_G, HALF // STAGES_R
    ex = [(send_x, mid_x, xs, s, s * wx, wx) for s in range(STAGES_X)]
    eg = [(send_g, mid_g, gs_, STAGES_X + s, ORDER_G[s], wg) for s in range(STAGES_G)]
    er = [(send_x, mid_x, send_g, STAGES_X + STAGES_G + s, s * wr, wr) for s in range(STAGES_R)]

    def activate(m):
        rows = jnp.concatenate([xs[b, m].reshape(256, QUARTER) for b in range(4)], axis=1)
        r = pl.ds(pl.multiple_of(m * 256, 256), 256)
        gate = dot(rows, win[0], 1, 0) * scale_in
        up = dot(rows, win[1], 1, 0) * scale_in
        sig = jax.nn.sigmoid(gate)
        act = gate * sig
        hid[r, :] = (act * up).astype(BF16)
        act_a[r, :] = up * sig * (1.0 + gate * (1.0 - sig))
        act_s[r, :] = act

    def out_copy(s, half):
        col = half * HALF + ORDER_G[s]
        q, off = col // QUARTER, col % QUARTER
        return q, pltpu.make_async_remote_copy(
            src_ref=grad_s.at[2, q, :, pl.ds(off, wg)],
            dst_ref=grad_r.at[z, 2, :, pl.ds(off, wg)],
            send_sem=rs_send.at[2, s, half],
            recv_sem=rs_recv.at[2 + off // wg, lax.rem(q - z + 4, 4)],
            device_id=(q, e), device_id_type=MESH,
        ), pltpu.make_async_copy(
            grad_s.at[2, q, :, pl.ds(off, wg)], grad_r.at[z, 2, :, pl.ds(off, wg)], rs_self.at[2, s, half]
        )

    def grad_out(s):
        for half in range(2):
            col = half * HALF + ORDER_G[s]
            q, off = col // QUARTER, col % QUARTER
            rows = gs_[:, :, :, :, col : col + wg].reshape(ROWS, wg)
            grad_s[2, q, :, off : off + wg] = (dot(hid[...], rows, 0, 0) * scale_out).astype(BF16)
            q, remote, local = out_copy(s, half)

            @pl.when(z != q)
            def _():
                remote.start()

            @pl.when(z == q)
            def _():
                local.start()

    def hidden_grad(s):
        def step(m, _):
            r = pl.ds(pl.multiple_of(m * 256, 256), 256)
            acc = None
            for half in range(2):
                col = half * HALF + ORDER_G[s]
                rows = gs_[m, :, :, :, col : col + wg].reshape(256, wg)
                part = dot(rows, wout[:, col : col + wg], 1, 1)
                acc = part if acc is None else acc + part
            if s > 0:
                acc = acc + dh[r, :]
            if s < STAGES_G - 1:
                dh[r, :] = acc
            else:
                acc = acc * scale_out
                dgu[0, r, :] = (acc * act_a[r, :]).astype(BF16)
                dgu[1, r, :] = (acc * act_s[r, :]).astype(BF16)
            return 0

        lax.fori_loop(0, 4, step, 0)

    def in_copy(mat, k):
        q = lax.rem(z + k, 4)
        return pltpu.make_async_remote_copy(
            src_ref=grad_s.at[mat, q], dst_ref=grad_r.at[z, mat],
            send_sem=rs_send.at[mat, k, 0], recv_sem=rs_recv.at[mat, k],
            device_id=(q, e), device_id_type=MESH,
        )

    def in_self(mat):
        return pltpu.make_async_copy(grad_s.at[mat, z], grad_r.at[z, mat], rs_self.at[mat, 0, 0])

    def grad_in(mat):
        def step(j, _):
            k = lax.rem(2 + 3 * j, 4)
            q = lax.rem(z + k, 4)
            rows = xs[q].reshape(ROWS, QUARTER)
            grad_s[mat, q] = (dot(rows, dgu[mat], 0, 0) * scale_in).astype(BF16)

            @pl.when(k != 0)
            def _():
                in_copy(mat, k).start()

            @pl.when(k == 0)
            def _():
                in_self(mat).start()

            return 0

        lax.fori_loop(0, 4, step, 0)

    def rows_back(s):
        def step(m, _):
            r = pl.ds(pl.multiple_of(m * 256, 256), 256)
            for half in range(2):
                col = half * HALF + s * wr
                v = dot(dgu[0, r, :], win[0, col : col + wr, :], 1, 1)
                v = v + dot(dgu[1, r, :], win[1, col : col + wr, :], 1, 1)
                send_x[m, :, :, :, col : col + wr] = (v * scale_in).astype(BF16).reshape(4, 2, CAP, wr)
            return 0

        lax.fori_loop(0, 4, step, 0)

    pairs = [(0, 0), (1, 1), (2, 2), (3, 3), (0, 1), (0, 2), (0, 3), (1, 2), (1, 3), (2, 3)]

    def fold(v):
        total = None
        for i in range(v.shape[0] // 8):
            for j in range(v.shape[1] // 128):
                part = v[i * 8 : (i + 1) * 8, j * 128 : (j + 1) * 128]
                total = part if total is None else total + part
        return total

    def gram_of(mat, sums):
        def step(i, sums):
            r = pl.ds(pl.multiple_of(i * 16, 16), 16)
            g = [grad_r[s, mat, r, :].astype(F32) for s in range(4)]
            return tuple(t + fold(g[a] * g[b]) for t, (a, b) in zip(sums, pairs))

        return lax.fori_loop(0, 32, step, sums)

    load[0].wait()
    gather(tok, send_x, ex[0][4], wx, False)
    pl.semaphore_wait(barrier, 16)
    start_first(ex[0])
    for copy in load[2:]:
        copy.start()
    gather(tok, send_x, ex[1][4], wx, False)
    start_first(ex[1])
    load[1].wait()
    gather(cot, send_g, eg[0][4], wg, True)
    gather(cot, send_g, eg[1][4], wg, True)
    forward(ex[0])
    start_first(eg[0])
    gather(cot, send_g, eg[2][4], wg, True)
    gather(cot, send_g, eg[3][4], wg, True)
    forward(ex[1])
    start_first(eg[1])
    forward(eg[0])
    start_first(eg[2])
    load[2].wait()
    load[3].wait()
    arrive(ex[0])
    arrive(ex[1])
    start_first(eg[3])
    each(0, 2, activate)
    forward(eg[1])
    each(2, 4, activate)
    forward(eg[2])
    arrive(eg[0])
    grad_out(0)
    hidden_grad(0)
    arrive(eg[1])
    grad_out(1)
    hidden_grad(1)
    forward(eg[3])
    arrive(eg[2])
    grad_out(2)
    hidden_grad(2)
    arrive(eg[3])
    grad_out(3)
    hidden_grad(3)
    grad_in(0)
    grad_in(1)
    for s in range(STAGES_R):
        rows_back(s)
        start_first(er[s])

    sums = tuple(jnp.zeros((8, 128), F32) for _ in pairs)
    for k in range(1, 4):
        for j in range(QUARTER // wg):
            pltpu.make_async_remote_copy(
                src_ref=grad_s.at[2, 0, :, pl.ds(j * wg, wg)],
                dst_ref=grad_r.at[lax.rem(z - k + 4, 4), 2, :, pl.ds(j * wg, wg)],
                send_sem=rs_send.at[2, 0, 0], recv_sem=rs_recv.at[2 + j, k],
                device_id=(lax.rem(z + k, 4), e), device_id_type=MESH,
            ).wait_recv()
    for s in range(STAGES_G):
        for half in range(2):
            q, remote, local = out_copy(s, half)

            @pl.when(z != q)
            def _():
                remote.wait_send()

            @pl.when(z == q)
            def _():
                local.wait()

    sums = gram_of(2, sums)
    for s in range(STAGES_R):
        forward(er[s])
    for mat in range(2):
        each(1, 4, lambda k: in_copy(mat, k).wait())
        in_self(mat).wait()
        sums = gram_of(mat, sums)

    own = jnp.concatenate([jnp.sum(t, axis=0, keepdims=True) for t in sums] + [jnp.zeros((6, 128), F32)], axis=0)
    gram[z] = own

    def gram_copy(k):
        return pltpu.make_async_remote_copy(
            src_ref=gram.at[z], dst_ref=gram.at[z], send_sem=gram_send.at[k], recv_sem=gram_recv.at[k],
            device_id=(lax.rem(z + k, 4), e), device_id_type=MESH,
        )

    each(1, 4, lambda k: gram_copy(k).start())
    load[4].wait()
    load[5].wait()
    each(1, 4, lambda k: gram_copy(k).wait())
    total = jnp.sum(gram[0] + gram[1] + gram[2] + gram[3], axis=1, keepdims=True)
    dots = {p: total[i : i + 1, :] for i, p in enumerate(pairs)}

    def coefficient(cross, norm):
        return 1.0 - cross / (2.0 * (norm + EPS))

    a0 = coefficient(dots[0, 2], dots[0, 0])
    a2 = coefficient(dots[0, 2], dots[2, 2])
    a1 = coefficient(dots[1, 3], dots[1, 1])
    a3 = coefficient(dots[1, 3], dots[3, 3])
    n0 = a0 * a0 * dots[0, 0] + 2.0 * a0 * a2 * dots[0, 2] + a2 * a2 * dots[2, 2]
    n1 = a1 * a1 * dots[1, 1] + 2.0 * a1 * a3 * dots[1, 3] + a3 * a3 * dots[3, 3]
    cross = a0 * (a1 * dots[0, 1] + a3 * dots[0, 3]) + a2 * (a1 * dots[1, 2] + a3 * dots[2, 3])
    b0 = coefficient(cross, jnp.maximum(n0, 0.0))
    b1 = coefficient(cross, jnp.maximum(n1, 0.0))
    coef = [b0 * a0, b1 * a1, b0 * a2, b1 * a3]

    def slot(mat, hh, owner):
        if mat < 2:
            return xs.at[2 * mat + owner // 2, 2 * lax.rem(owner, 2) + hh]
        return nwout.at[pl.ds(hh * 256, 256), pl.ds(pl.multiple_of(owner * QUARTER, QUARTER), QUARTER)]

    def ag_copy(mat, hh, direction):
        return pltpu.make_async_remote_copy(
            src_ref=slot(mat, hh, z), dst_ref=slot(mat, hh, z),
            send_sem=ag_send.at[direction, 2 * mat + hh], recv_sem=ag_recv.at[direction, 2 * mat + hh],
            device_id=(lax.rem(z + (1 if direction == 0 else 3), 4), e), device_id_type=MESH,
        )

    def fw_copy(mat, hh):
        owner = lax.rem(z + (3 if hh == 0 else 1), 4)
        return pltpu.make_async_remote_copy(
            src_ref=slot(mat, hh, owner), dst_ref=slot(mat, hh, owner),
            send_sem=fw_send.at[2 * mat + hh], recv_sem=fw_recv.at[2 * mat + hh],
            device_id=(lax.rem(z + (1 if hh == 0 else 3), 4), e), device_id_type=MESH,
        )

    for mat in range(3):
        for hh in range(2):

            def step(i, _):
                r = pl.multiple_of(hh * 256 + i * 32, 32)
                rr = pl.ds(r, 32)
                comb = coef[0] * grad_r[0, mat, rr, :].astype(F32)
                for s in range(1, 4):
                    comb = comb + coef[s] * grad_r[s, mat, rr, :].astype(F32)
                if mat < 2:
                    new = MOMENTUM * mom_in[mat, rr, :] + comb
                    mom_in[mat, rr, :] = new
                    old = win[mat, pl.ds(pl.multiple_of(z * QUARTER + r, 32), 32), :]
                else:
                    new = MOMENTUM * mom_out[rr, :] + comb
                    mom_out[rr, :] = new
                    old = wout[rr, pl.ds(pl.multiple_of(z * QUARTER, QUARTER), QUARTER)]
                value = (old.astype(F32) - RATE * new).astype(BF16)
                if mat < 2:
                    xs[2 * mat + z // 2, 2 * lax.rem(z, 2) + hh, i // 2, lax.rem(i, 2)] = value
                else:
                    nwout[rr, pl.ds(pl.multiple_of(z * QUARTER, QUARTER), QUARTER)] = value
                return 0

            lax.fori_loop(0, 8, step, 0)
            ag_copy(mat, hh, 0).start()
            ag_copy(mat, hh, 1).start()

    def pass_on(mat, hh):
        ag_copy(mat, hh, hh).wait_recv()
        fw_copy(mat, hh).start()

    pass_on(0, 0)
    pass_on(0, 1)

    for s in range(STAGES_R):
        arrive(er[s])

    def tokens_step(n, _):
        cols = pl.ds(pl.multiple_of(n * 512, 512), 512)
        rows = send_g[:, :, :, :, cols].reshape(ROWS, 512)
        tok[:, cols] = dot(onehot[...], rows, 0, 0).astype(BF16)
        return 0

    lax.fori_loop(0, 4, tokens_step, 0)

    for mat in range(1, 3):
        for hh in range(2):
            pass_on(mat, hh)
    for mat in range(3):
        for hh in range(2):
            ag_copy(mat, hh, 1 - hh).wait_recv()
            ag_copy(mat, hh, 0).wait_send()
            ag_copy(mat, hh, 1).wait_send()
            fw_copy(mat, hh).wait()


def shards(tokens, cotangent, slot_rows, slot_count, slot_weight, w_in, w_out, momentum_in, momentum_out):
    any_ = pl.BlockSpec(memory_space=pl.ANY)
    vmem = pl.BlockSpec(memory_space=pltpu.VMEM)
    stages = STAGES_X + STAGES_G + STAGES_R
    grid5 = (4, 4, 2, CAP, D)
    mid = (2, 4, 4, 2, CAP, HALF)
    dma = pltpu.SemaphoreType.DMA
    outs = pl.pallas_call(
        kernel,
        out_shape=(
            pltpu.VMEM((256, D), BF16),
            pltpu.VMEM((4, 4, 4, 2, CAP, QUARTER), BF16),
            pltpu.VMEM((FF, D), BF16),
            pltpu.VMEM((2, QUARTER, FF), F32),
            pltpu.VMEM((FF, QUARTER), F32),
        ),
        in_specs=[any_, any_, vmem, vmem, vmem, any_, any_, any_, any_],
        out_specs=(vmem,) * 5,
        scratch_shapes=[
            pltpu.VMEM((256, D), BF16),
            pltpu.VMEM((ROWS, 256), BF16),
            pltpu.VMEM((ROWS, 128), F32),
            pltpu.VMEM(grid5, BF16),
            pltpu.VMEM(grid5, BF16),
            pltpu.VMEM(mid, BF16),
            pltpu.VMEM(mid, BF16),
            pltpu.VMEM(grid5, BF16),
            pltpu.VMEM((2, D, FF), BF16),
            pltpu.VMEM((FF, D), BF16),
            pltpu.VMEM((ROWS, FF), F32),
            pltpu.VMEM((ROWS, FF), F32),
            pltpu.VMEM((ROWS, FF), BF16),
            pltpu.VMEM((ROWS, FF), F32),
            pltpu.VMEM((2, ROWS, FF), BF16),
            pltpu.VMEM((3, 4, QUARTER, QUARTER), BF16),
            pltpu.VMEM((4, 3, QUARTER, QUARTER), BF16),
            pltpu.VMEM((4, 16, 128), F32),
            dma((6,)),
            dma((stages, 2, 8)),
            dma((stages, 2, 8)),
            dma((stages, 2, 4)),
            dma((stages, 2, 4)),
            dma((stages, 2)),
            dma((stages, 2)),
            dma((3, STAGES_G, 2)),
            dma((4, 4)),
            dma((3, STAGES_G, 2)),
            dma((4,)),
            dma((4,)),
            dma((2, 6)),
            dma((2, 6)),
            dma((6,)),
            dma((6,)),
        ],
        compiler_params=pltpu.CompilerParams(
            collective_id=0, has_side_effects=True, vmem_limit_bytes=53 << 20
        ),
        name="step",
    )(
        tokens[0], cotangent[0], slot_rows[0, 0], slot_count[0], slot_weight[0, 0],
        w_in[0], w_out[0], momentum_in[0], momentum_out[0],
    )
    outs = (outs[0], outs[1].reshape(2, D, FF)) + tuple(outs[2:])
    return tuple(o[None] for o in outs)


def solution(mesh):
    return jax.shard_map(
        shards,
        mesh=mesh,
        in_specs=(
            P("dp", "expert", None),
            P("dp", "expert", None),
            P("dp", "expert", None, None),
            P("dp", "expert", None),
            P("dp", "expert", None, None),
            P("expert", None, None, None),
            P("expert", None, None),
            P("expert", None, "dp", None),
            P("expert", None, "dp"),
        ),
        out_specs=(
            P("dp", "expert", None),
            P("expert", None, None, None),
            P("expert", None, None),
            P("expert", None, "dp", None),
            P("expert", None, "dp"),
        ),
        check_vma=False,
    )
```

```python
import jax
import jax.numpy as jnp
from jax import lax
from jax.experimental import pallas as pl
from jax.experimental.pallas import tpu as pltpu
from jax.sharding import PartitionSpec as P

EPS = 1e-06
MOMENTUM = 0.9
RATE = 0.1
MESH = pl.DeviceIdType.MESH

D = 2048
FF = 512
HALF = 1024
QUARTER = 512
CAP = 32
STAGES_X = 2
STAGES_G = 4
STAGES_R = 2
ROWS = 1024
BF16 = jnp.bfloat16
F32 = jnp.float32


def dot(a, b, ca, cb):
    return lax.dot_general(a, b, (((ca,), (cb,)), ((), ())), preferred_element_type=F32)


def kernel(
    tok_h, cot_h, rows_v, count_v, weight_v, win_h, wout_h, min_h, mout_h,
    tok, xs, nwout, mom_in, mom_out,
    cot, onehot, scale, send_x, send_g, mid_x, mid_g, gs_, win, wout,
    act_a, act_s, hid, dh, dgu, grad_s, grad_r, gram,
    load_sem, p1_send, p1_recv, p2_send, p2_recv, self1, self2,
    rs_send, rs_recv, rs_self, gram_send, gram_recv, ag_send, ag_recv, fw_send, fw_recv,
):
    z = lax.axis_index("dp")
    e = lax.axis_index("expert")
    x = e // 8
    y = lax.rem(e // 2, 4)
    c = lax.rem(e, 2)
    scale_in = D ** (-0.5)
    scale_out = FF ** (-0.5)

    def expert_id(px, py, pc):
        return (px * 4 + py) * 2 + pc

    loads = [
        (tok_h, tok), (cot_h, cot), (win_h, win), (wout_h, wout), (min_h, mom_in), (mout_h, mom_out),
    ]
    load = [pltpu.make_async_copy(s, d, load_sem.at[i]) for i, (s, d) in enumerate(loads)]
    for copy in load[:2]:
        copy.start()

    barrier = pltpu.get_barrier_semaphore()

    def greet(device):
        pl.semaphore_signal(barrier, inc=1, device_id=device, device_id_type=MESH)

    for k in range(1, 8):
        greet((z, expert_id(lax.rem(x + k // 2, 4), y, lax.rem(c + k % 2, 2))))
    for k in range(2, 8):
        greet((z, expert_id(x, lax.rem(y + k // 2, 4), lax.rem(c + k % 2, 2))))
    for k in range(1, 4):
        greet((lax.rem(z + k, 4), e))

    rows_t = jnp.transpose(rows_v[...])
    weight_t = jnp.transpose(weight_v[...])
    valid = lax.broadcasted_iota(jnp.int32, (CAP, 32), 0) < count_v[...]
    scale_t = jnp.where(valid, weight_t, 0.0)
    lane = lax.broadcasted_iota(jnp.int32, (CAP, 256), 1)
    for k in range(32):
        onehot[k * CAP : (k + 1) * CAP, :] = (lane == rows_t[:, k : k + 1]).astype(F32).astype(BF16)
        scale[k * CAP : (k + 1) * CAP, :] = jnp.broadcast_to(scale_t[:, k : k + 1], (CAP, 128))

    def gather(src, dst, c0, w, scaled):
        def step(m, _):
            r0 = pl.multiple_of(m * 256, 256)
            hot = onehot[pl.ds(r0, 256), :]
            if scaled:
                for q in range(4):
                    v = dot(hot, src[:, q * QUARTER + c0 : q * QUARTER + c0 + w], 1, 0)
                    v = v * scale[pl.ds(r0, 256), 0:1]
                    dst[q, m, :, :, :, c0 : c0 + w] = v.astype(BF16).reshape(4, 2, CAP, w)
            else:
                for half in range(2):
                    col = half * HALF + c0
                    v = dot(hot, src[:, col : col + w], 1, 0)
                    dst[m, :, :, :, col : col + w] = v.astype(BF16).reshape(4, 2, CAP, w)
            return 0

        lax.fori_loop(0, 4, step, 0)

    def first_views(send, mid, c0, w, half, pa, pc):
        if send is send_g:
            col, both = pl.ds(c0, w), pl.ds(2 * half, 2)
            if half == 0:
                return send.at[both, pa, :, pc, :, col], mid.at[0, :, :, x, c, :, col]
            return send.at[both, :, pa, pc, :, col], mid.at[1, :, :, y, c, :, col]
        col, mcol = pl.ds(half * HALF + c0, w), pl.ds(c0, w)
        if half == 0:
            return send.at[pa, :, pc, :, col], mid.at[0, :, x, c, :, mcol]
        return send.at[:, pa, pc, :, col], mid.at[1, :, y, c, :, mcol]

    def second_views(mid, fin, c0, w, half, pa):
        if mid is mid_g:
            col, both = pl.ds(c0, w), pl.ds(2 * half, 2)
            src = mid.at[half, :, pa, :, :, :, col]
            if half == 0:
                return src, fin.at[both, :, y, :, :, col]
            return src, fin.at[both, x, :, :, :, col]
        src = mid.at[half, pa, :, :, :, pl.ds(c0, w)]
        if half == 0:
            return src, fin.at[c0 // QUARTER, :, y]
        return src, fin.at[2 + c0 // QUARTER, x]

    def p1_copy(send, mid, st, c0, w, half, k):
        pc = lax.rem(c + lax.rem(k, 2), 2)
        pa = lax.rem((x if half == 0 else y) + k // 2, 4)
        peer = expert_id(pa, y, pc) if half == 0 else expert_id(x, pa, pc)
        src, dst = first_views(send, mid, c0, w, half, pa, pc)
        return pltpu.make_async_remote_copy(
            src_ref=src, dst_ref=dst, send_sem=p1_send.at[st, half, k], recv_sem=p1_recv.at[st, half, k],
            device_id=(z, peer), device_id_type=MESH,
        )

    def p1_self(send, mid, st, c0, w, half):
        src, dst = first_views(send, mid, c0, w, half, x if half == 0 else y, c)
        return pltpu.make_async_copy(src, dst, self1.at[st, half])

    def p2_copy(mid, fin, st, c0, w, half, k):
        pa = lax.rem((y if half == 0 else x) + k, 4)
        peer = expert_id(x, pa, c) if half == 0 else expert_id(pa, y, c)
        src, dst = second_views(mid, fin, c0, w, half, pa)
        return pltpu.make_async_remote_copy(
            src_ref=src, dst_ref=dst, send_sem=p2_send.at[st, half, k], recv_sem=p2_recv.at[st, half, k],
            device_id=(z, peer), device_id_type=MESH,
        )

    def p2_self(mid, fin, st, c0, w, half):
        src, dst = second_views(mid, fin, c0, w, half, y if half == 0 else x)
        return pltpu.make_async_copy(src, dst, self2.at[st, half])

    def each(lo, hi, fn):
        def step(k, _):
            fn(k)
            return 0

        lax.fori_loop(lo, hi, step, 0)

    def start_first(args):
        send, mid, fin, st, c0, w = args

        def go(k):
            p1_copy(send, mid, st, c0, w, 0, k).start()
            p1_copy(send, mid, st, c0, w, 1, k).start()

        each(1, 8, go)
        for half in range(2):
            p1_self(send, mid, st, c0, w, half).start()

    def forward(args):
        send, mid, fin, st, c0, w = args
        for half in range(2):
            each(1, 8, lambda k: p1_copy(send, mid, st, c0, w, half, k).wait())
            p1_self(send, mid, st, c0, w, half).wait()
            each(1, 4, lambda k: p2_copy(mid, fin, st, c0, w, half, k).start())
            p2_self(mid, fin, st, c0, w, half).start()

    def arrive(args):
        send, mid, fin, st, c0, w = args
        for half in range(2):
            each(1, 4, lambda k: p2_copy(mid, fin, st, c0, w, half, k).wait())
            p2_self(mid, fin, st, c0, w, half).wait()

    wx, wg, wr = HALF // STAGES_X, QUARTER // STAGES_G, HALF // STAGES_R
    ex = [(send_x, mid_x, xs, s, s * wx, wx) for s in range(STAGES_X)]
    eg = [(send_g, mid_g, gs_, STAGES_X + s, s * wg, wg) for s in range(STAGES_G)]
    er = [(send_x, mid_x, send_g, STAGES_X + STAGES_G + s, s * wr, wr) for s in range(STAGES_R)]

    def activate(m):
        rows = jnp.concatenate([xs[b, m].reshape(256, QUARTER) for b in range(4)], axis=1)
        r = pl.ds(pl.multiple_of(m * 256, 256), 256)
        gate = dot(rows, win[0], 1, 0) * scale_in
        up = dot(rows, win[1], 1, 0) * scale_in
        sig = jax.nn.sigmoid(gate)
        act = gate * sig
        hid[r, :] = (act * up).astype(BF16)
        act_a[r, :] = up * sig * (1.0 + gate * (1.0 - sig))
        act_s[r, :] = act

    def out_copy(s, q):
        src = grad_s.at[2, q, :, pl.ds(s * wg, wg)]
        dst = grad_r.at[z, 2, :, pl.ds(s * wg, wg)]
        return pltpu.make_async_remote_copy(
            src_ref=src, dst_ref=dst, send_sem=rs_send.at[2 + s, q],
            recv_sem=rs_recv.at[2 + s, lax.rem(q - z + 4, 4)], device_id=(q, e), device_id_type=MESH,
        ), pltpu.make_async_copy(src, dst, rs_self.at[2 + s])

    def grad_out(s):
        cols = slice(s * wg, s * wg + wg)
        rows = jnp.concatenate([gs_[q, :, :, :, :, cols].reshape(ROWS, wg) for q in range(4)], axis=1)
        out = (dot(hid[...], rows, 0, 0) * scale_out).astype(BF16)
        for q in range(4):
            grad_s[2, q, :, cols] = out[:, q * wg : (q + 1) * wg]
            remote, local = out_copy(s, q)

            @pl.when(z != q)
            def _():
                remote.start()

            @pl.when(z == q)
            def _():
                local.start()

    def hidden_grad(s):
        def step(m, _):
            r = pl.ds(pl.multiple_of(m * 256, 256), 256)
            cols = slice(s * wg, s * wg + wg)
            rows = jnp.concatenate([gs_[q, m, :, :, :, cols].reshape(256, wg) for q in range(4)], axis=1)
            down = jnp.concatenate(
                [wout[:, q * QUARTER + s * wg : q * QUARTER + s * wg + wg] for q in range(4)], axis=1
            )
            acc = dot(rows, down, 1, 1)
            if s > 0:
                acc = acc + dh[r, :]
            if s < STAGES_G - 1:
                dh[r, :] = acc
            else:
                acc = acc * scale_out
                dgu[0, r, :] = (acc * act_a[r, :]).astype(BF16)
                dgu[1, r, :] = (acc * act_s[r, :]).astype(BF16)
            return 0

        lax.fori_loop(0, 4, step, 0)

    def in_copy(mat, k):
        q = lax.rem(z + k, 4)
        return pltpu.make_async_remote_copy(
            src_ref=grad_s.at[mat, q], dst_ref=grad_r.at[z, mat],
            send_sem=rs_send.at[mat, k], recv_sem=rs_recv.at[mat, k],
            device_id=(q, e), device_id_type=MESH,
        )

    def in_self(mat):
        return pltpu.make_async_copy(grad_s.at[mat, z], grad_r.at[z, mat], rs_self.at[mat])

    def grad_in(mat):
        def step(j, _):
            k = lax.rem(2 + 3 * j, 4)
            q = lax.rem(z + k, 4)
            rows = xs[q].reshape(ROWS, QUARTER)
            grad_s[mat, q] = (dot(rows, dgu[mat], 0, 0) * scale_in).astype(BF16)

            @pl.when(k != 0)
            def _():
                in_copy(mat, k).start()

            @pl.when(k == 0)
            def _():
                in_self(mat).start()

            return 0

        lax.fori_loop(0, 4, step, 0)

    def rows_back(s):
        def step(m, _):
            r = pl.ds(pl.multiple_of(m * 256, 256), 256)
            for half in range(2):
                col = half * HALF + s * wr
                v = dot(dgu[0, r, :], win[0, col : col + wr, :], 1, 1)
                v = v + dot(dgu[1, r, :], win[1, col : col + wr, :], 1, 1)
                send_x[m, :, :, :, col : col + wr] = (v * scale_in).astype(BF16).reshape(4, 2, CAP, wr)
            return 0

        lax.fori_loop(0, 4, step, 0)

    pairs = [(0, 0), (1, 1), (2, 2), (3, 3), (0, 1), (0, 2), (0, 3), (1, 2), (1, 3), (2, 3)]

    def fold(v):
        total = None
        for i in range(v.shape[0] // 8):
            for j in range(v.shape[1] // 128):
                part = v[i * 8 : (i + 1) * 8, j * 128 : (j + 1) * 128]
                total = part if total is None else total + part
        return total

    def gram_of(mat, sums):
        def step(i, sums):
            r = pl.ds(pl.multiple_of(i * 16, 16), 16)
            g = [grad_r[s, mat, r, :].astype(F32) for s in range(4)]
            return tuple(t + fold(g[a] * g[b]) for t, (a, b) in zip(sums, pairs))

        return lax.fori_loop(0, 32, step, sums)

    load[0].wait()
    gather(tok, send_x, ex[0][4], wx, False)
    pl.semaphore_wait(barrier, 16)
    start_first(ex[0])
    for copy in load[2:]:
        copy.start()
    gather(tok, send_x, ex[1][4], wx, False)
    start_first(ex[1])
    load[1].wait()
    gather(cot, send_g, eg[0][4], wg, True)
    gather(cot, send_g, eg[1][4], wg, True)
    forward(ex[0])
    start_first(eg[0])
    gather(cot, send_g, eg[2][4], wg, True)
    gather(cot, send_g, eg[3][4], wg, True)
    forward(ex[1])
    start_first(eg[1])
    forward(eg[0])
    start_first(eg[2])
    load[2].wait()
    load[3].wait()
    arrive(ex[0])
    arrive(ex[1])
    start_first(eg[3])
    each(0, 2, activate)
    forward(eg[1])
    each(2, 4, activate)
    forward(eg[2])
    arrive(eg[0])
    grad_out(0)
    hidden_grad(0)
    arrive(eg[1])
    grad_out(1)
    hidden_grad(1)
    forward(eg[3])
    arrive(eg[2])
    grad_out(2)
    hidden_grad(2)
    arrive(eg[3])
    grad_out(3)
    hidden_grad(3)
    grad_in(0)
    grad_in(1)
    for s in range(STAGES_R):
        rows_back(s)
        start_first(er[s])

    sums = tuple(jnp.zeros((8, 128), F32) for _ in pairs)
    for k in range(1, 4):
        for j in range(STAGES_G):
            pltpu.make_async_remote_copy(
                src_ref=grad_s.at[2, 0, :, pl.ds(j * wg, wg)],
                dst_ref=grad_r.at[lax.rem(z - k + 4, 4), 2, :, pl.ds(j * wg, wg)],
                send_sem=rs_send.at[2 + j, k], recv_sem=rs_recv.at[2 + j, k],
                device_id=(lax.rem(z + k, 4), e), device_id_type=MESH,
            ).wait_recv()
    for s in range(STAGES_G):
        for q in range(4):
            remote, local = out_copy(s, q)

            @pl.when(z != q)
            def _():
                remote.wait_send()

            @pl.when(z == q)
            def _():
                local.wait()

    sums = gram_of(2, sums)
    for s in range(STAGES_R):
        forward(er[s])
    for mat in range(2):
        each(1, 4, lambda k: in_copy(mat, k).wait())
        in_self(mat).wait()
        sums = gram_of(mat, sums)

    own = jnp.concatenate([jnp.sum(t, axis=0, keepdims=True) for t in sums] + [jnp.zeros((6, 128), F32)], axis=0)
    gram[z] = own

    def gram_copy(k):
        return pltpu.make_async_remote_copy(
            src_ref=gram.at[z], dst_ref=gram.at[z], send_sem=gram_send.at[k], recv_sem=gram_recv.at[k],
            device_id=(lax.rem(z + k, 4), e), device_id_type=MESH,
        )

    each(1, 4, lambda k: gram_copy(k).start())
    load[4].wait()
    load[5].wait()
    each(1, 4, lambda k: gram_copy(k).wait())
    total = jnp.sum(gram[0] + gram[1] + gram[2] + gram[3], axis=1, keepdims=True)
    dots = {p: total[i : i + 1, :] for i, p in enumerate(pairs)}

    def coefficient(cross, norm):
        return 1.0 - cross / (2.0 * (norm + EPS))

    a0 = coefficient(dots[0, 2], dots[0, 0])
    a2 = coefficient(dots[0, 2], dots[2, 2])
    a1 = coefficient(dots[1, 3], dots[1, 1])
    a3 = coefficient(dots[1, 3], dots[3, 3])
    n0 = a0 * a0 * dots[0, 0] + 2.0 * a0 * a2 * dots[0, 2] + a2 * a2 * dots[2, 2]
    n1 = a1 * a1 * dots[1, 1] + 2.0 * a1 * a3 * dots[1, 3] + a3 * a3 * dots[3, 3]
    cross = a0 * (a1 * dots[0, 1] + a3 * dots[0, 3]) + a2 * (a1 * dots[1, 2] + a3 * dots[2, 3])
    b0 = coefficient(cross, jnp.maximum(n0, 0.0))
    b1 = coefficient(cross, jnp.maximum(n1, 0.0))
    coef = [b0 * a0, b1 * a1, b0 * a2, b1 * a3]

    def slot(mat, hh, owner):
        if mat < 2:
            return xs.at[2 * mat + owner // 2, 2 * lax.rem(owner, 2) + hh]
        return nwout.at[pl.ds(hh * 256, 256), pl.ds(pl.multiple_of(owner * QUARTER, QUARTER), QUARTER)]

    def ag_copy(mat, hh, direction):
        return pltpu.make_async_remote_copy(
            src_ref=slot(mat, hh, z), dst_ref=slot(mat, hh, z),
            send_sem=ag_send.at[direction, 2 * mat + hh], recv_sem=ag_recv.at[direction, 2 * mat + hh],
            device_id=(lax.rem(z + (1 if direction == 0 else 3), 4), e), device_id_type=MESH,
        )

    def fw_copy(mat, hh):
        owner = lax.rem(z + (3 if hh == 0 else 1), 4)
        return pltpu.make_async_remote_copy(
            src_ref=slot(mat, hh, owner), dst_ref=slot(mat, hh, owner),
            send_sem=fw_send.at[2 * mat + hh], recv_sem=fw_recv.at[2 * mat + hh],
            device_id=(lax.rem(z + (1 if hh == 0 else 3), 4), e), device_id_type=MESH,
        )

    for mat in range(3):
        for hh in range(2):

            def step(i, _):
                r = pl.multiple_of(hh * 256 + i * 32, 32)
                rr = pl.ds(r, 32)
                comb = coef[0] * grad_r[0, mat, rr, :].astype(F32)
                for s in range(1, 4):
                    comb = comb + coef[s] * grad_r[s, mat, rr, :].astype(F32)
                if mat < 2:
                    new = MOMENTUM * mom_in[mat, rr, :] + comb
                    mom_in[mat, rr, :] = new
                    old = win[mat, pl.ds(pl.multiple_of(z * QUARTER + r, 32), 32), :]
                else:
                    new = MOMENTUM * mom_out[rr, :] + comb
                    mom_out[rr, :] = new
                    old = wout[rr, pl.ds(pl.multiple_of(z * QUARTER, QUARTER), QUARTER)]
                value = (old.astype(F32) - RATE * new).astype(BF16)
                if mat < 2:
                    xs[2 * mat + z // 2, 2 * lax.rem(z, 2) + hh, i // 2, lax.rem(i, 2)] = value
                else:
                    nwout[rr, pl.ds(pl.multiple_of(z * QUARTER, QUARTER), QUARTER)] = value
                return 0

            lax.fori_loop(0, 8, step, 0)
            ag_copy(mat, hh, 0).start()
            ag_copy(mat, hh, 1).start()

    def pass_on(mat, hh):
        ag_copy(mat, hh, hh).wait_recv()
        fw_copy(mat, hh).start()

    pass_on(0, 0)
    pass_on(0, 1)

    for s in range(STAGES_R):
        arrive(er[s])

    def tokens_step(n, _):
        cols = pl.ds(pl.multiple_of(n * 512, 512), 512)
        rows = send_g[n].reshape(ROWS, 512)
        tok[:, cols] = dot(onehot[...], rows, 0, 0).astype(BF16)
        return 0

    lax.fori_loop(0, 4, tokens_step, 0)

    for mat in range(1, 3):
        for hh in range(2):
            pass_on(mat, hh)
    for mat in range(3):
        for hh in range(2):
            ag_copy(mat, hh, 1 - hh).wait_recv()
            ag_copy(mat, hh, 0).wait_send()
            ag_copy(mat, hh, 1).wait_send()
            fw_copy(mat, hh).wait()


def write_out(*refs):
    sources, targets, sem = refs[:5], refs[5:10], refs[10]
    copies = []
    for source, target in zip(sources, targets):
        parts = source.shape[0] if len(source.shape) != 2 else 2
        rows = source.shape[0] // parts
        for part in range(parts):
            at = pl.ds(part * rows, rows)
            copies.append(pltpu.make_async_copy(source.at[at], target.at[at], sem.at[len(copies)]))
    for copy in copies:
        copy.start()
    for copy in copies:
        copy.wait()


def shards(tokens, cotangent, slot_rows, slot_count, slot_weight, w_in, w_out, momentum_in, momentum_out):
    any_ = pl.BlockSpec(memory_space=pl.ANY)
    vmem = pl.BlockSpec(memory_space=pltpu.VMEM)
    stages = STAGES_X + STAGES_G + STAGES_R
    grid5 = (4, 4, 2, CAP, D)
    mid = (2, 4, 4, 2, CAP, HALF)
    blocks = (4, 4, 4, 2, CAP, QUARTER)
    mid_blocks = (2, 2, 4, 4, 2, CAP, QUARTER)
    dma = pltpu.SemaphoreType.DMA
    outs = pl.pallas_call(
        kernel,
        out_shape=(
            pltpu.VMEM((256, D), BF16),
            pltpu.VMEM(blocks, BF16),
            pltpu.VMEM((FF, D), BF16),
            pltpu.VMEM((2, QUARTER, FF), F32),
            pltpu.VMEM((FF, QUARTER), F32),
        ),
        in_specs=[any_, any_, vmem, vmem, vmem, any_, any_, any_, any_],
        out_specs=(vmem,) * 5,
        scratch_shapes=[
            pltpu.VMEM((256, D), BF16),
            pltpu.VMEM((ROWS, 256), BF16),
            pltpu.VMEM((ROWS, 128), F32),
            pltpu.VMEM(grid5, BF16),
            pltpu.VMEM(blocks, BF16),
            pltpu.VMEM(mid, BF16),
            pltpu.VMEM(mid_blocks, BF16),
            pltpu.VMEM(blocks, BF16),
            pltpu.VMEM((2, D, FF), BF16),
            pltpu.VMEM((FF, D), BF16),
            pltpu.VMEM((ROWS, FF), F32),
            pltpu.VMEM((ROWS, FF), F32),
            pltpu.VMEM((ROWS, FF), BF16),
            pltpu.VMEM((ROWS, FF), F32),
            pltpu.VMEM((2, ROWS, FF), BF16),
            pltpu.VMEM((3, 4, QUARTER, QUARTER), BF16),
            pltpu.VMEM((4, 3, QUARTER, QUARTER), BF16),
            pltpu.VMEM((4, 16, 128), F32),
            dma((6,)),
            dma((stages, 2, 8)),
            dma((stages, 2, 8)),
            dma((stages, 2, 4)),
            dma((stages, 2, 4)),
            dma((stages, 2)),
            dma((stages, 2)),
            dma((2 + STAGES_G, 4)),
            dma((2 + STAGES_G, 4)),
            dma((2 + STAGES_G,)),
            dma((4,)),
            dma((4,)),
            dma((2, 6)),
            dma((2, 6)),
            dma((6,)),
            dma((6,)),
        ],
        compiler_params=pltpu.CompilerParams(
            collective_id=0, has_side_effects=True, vmem_limit_bytes=53 << 20
        ),
        name="step",
    )(
        tokens[0], cotangent[0], slot_rows[0, 0], slot_count[0], slot_weight[0, 0],
        w_in[0], w_out[0], momentum_in[0], momentum_out[0],
    )
    outs = [pltpu.with_memory_space_constraint(o, pltpu.VMEM) for o in outs]
    outs = pl.pallas_call(
        write_out,
        out_shape=[pltpu.HBM(o.shape, o.dtype) for o in outs],
        in_specs=[vmem] * 5,
        out_specs=[pl.BlockSpec(memory_space=pltpu.HBM)] * 5,
        scratch_shapes=[dma((16,))],
        compiler_params=pltpu.CompilerParams(vmem_limit_bytes=1 << 20),
        name="write_out",
    )(*outs)
    outs = (outs[0], outs[1].reshape(2, D, FF)) + tuple(outs[2:])
    return tuple(o[None] for o in outs)


def solution(mesh):
    return jax.shard_map(
        shards,
        mesh=mesh,
        in_specs=(
            P("dp", "expert", None),
            P("dp", "expert", None),
            P("dp", "expert", None, None),
            P("dp", "expert", None),
            P("dp", "expert", None, None),
            P("expert", None, None, None),
            P("expert", None, None),
            P("expert", None, "dp", None),
            P("expert", None, "dp"),
        ),
        out_specs=(
            P("dp", "expert", None),
            P("expert", None, None, None),
            P("expert", None, None),
            P("expert", None, "dp", None),
            P("expert", None, "dp"),
        ),
        check_vma=False,
    )
```

```python
import jax
import jax.numpy as jnp
from jax import lax
from jax.experimental import pallas as pl
from jax.experimental.pallas import tpu as pltpu
from jax.sharding import PartitionSpec as P

EPS = 1e-06
MOMENTUM = 0.9
RATE = 0.1
MESH = pl.DeviceIdType.MESH

D = 2048
FF = 512
HALF = 1024
QUARTER = 512
CAP = 32
STAGES_X = 2
STAGES_G = 4
STAGES_R = 2
ROWS = 1024
BF16 = jnp.bfloat16
F32 = jnp.float32


def dot(a, b, ca, cb):
    return lax.dot_general(a, b, (((ca,), (cb,)), ((), ())), preferred_element_type=F32)


def kernel(
    tok_h, cot_h, rows_v, count_v, weight_v, win_h, wout_h, min_h, mout_h,
    tok, xs, nwout, mom_in, mom_out,
    cot, onehot, scale, send_x, send_g, mid_x, mid_g, gs_, win, wout,
    act_a, act_s, hid, dh, dgu, grad_s, grad_r, gram,
    load_sem, p1_send, p1_recv, p2_send, p2_recv,
    rs_send, rs_recv, gram_sem, ag_send, ag_recv, ag_last, fw_sem,
):
    z = lax.axis_index("dp")
    e = lax.axis_index("expert")
    x = e // 8
    y = lax.rem(e // 2, 4)
    c = lax.rem(e, 2)
    scale_in = D ** (-0.5)
    scale_out = FF ** (-0.5)

    def expert_id(px, py, pc):
        return (px * 4 + py) * 2 + pc

    loads = [
        (tok_h, tok), (cot_h, cot), (win_h, win), (wout_h, wout), (min_h, mom_in), (mout_h, mom_out),
    ]
    load = [pltpu.make_async_copy(s, d, load_sem.at[i]) for i, (s, d) in enumerate(loads)]
    for copy in load[:2]:
        copy.start()

    barrier = pltpu.get_barrier_semaphore()

    def greet(device):
        pl.semaphore_signal(barrier, inc=1, device_id=device, device_id_type=MESH)

    for k in range(1, 8):
        greet((z, expert_id(lax.rem(x + k // 2, 4), y, lax.rem(c + k % 2, 2))))
    for k in range(2, 8):
        greet((z, expert_id(x, lax.rem(y + k // 2, 4), lax.rem(c + k % 2, 2))))
    for k in range(1, 4):
        greet((lax.rem(z + k, 4), e))

    rows_t = jnp.transpose(rows_v[...])
    weight_t = jnp.transpose(weight_v[...])
    valid = lax.broadcasted_iota(jnp.int32, (CAP, 32), 0) < count_v[...]
    scale_t = jnp.where(valid, weight_t, 0.0)
    lane = lax.broadcasted_iota(jnp.int32, (CAP, 256), 1)
    for k in range(32):
        onehot[k * CAP : (k + 1) * CAP, :] = (lane == rows_t[:, k : k + 1]).astype(F32).astype(BF16)
        scale[k * CAP : (k + 1) * CAP, :] = jnp.broadcast_to(scale_t[:, k : k + 1], (CAP, 128))

    def gather(src, dst, c0, w, scaled):
        def step(m, _):
            r0 = pl.multiple_of(m * 256, 256)
            hot = onehot[pl.ds(r0, 256), :]
            if scaled:
                for q in range(4):
                    v = dot(hot, src[:, q * QUARTER + c0 : q * QUARTER + c0 + w], 1, 0)
                    v = v * scale[pl.ds(r0, 256), 0:1]
                    dst[q, m, :, :, :, c0 : c0 + w] = v.astype(BF16).reshape(4, 2, CAP, w)
            else:
                for half in range(2):
                    col = half * HALF + c0
                    v = dot(hot, src[:, col : col + w], 1, 0)
                    dst[m, :, :, :, col : col + w] = v.astype(BF16).reshape(4, 2, CAP, w)
            return 0

        lax.fori_loop(0, 4, step, 0)

    def first_views(send, mid, c0, w, half, pa, pc):
        if send is send_g:
            col, both = pl.ds(c0, w), pl.ds(2 * half, 2)
            if half == 0:
                return send.at[both, pa, :, pc, :, col], mid.at[0, :, :, x, c, :, col]
            return send.at[both, :, pa, pc, :, col], mid.at[1, :, :, y, c, :, col]
        col, mcol = pl.ds(half * HALF + c0, w), pl.ds(c0, w)
        if half == 0:
            return send.at[pa, :, pc, :, col], mid.at[0, :, x, c, :, mcol]
        return send.at[:, pa, pc, :, col], mid.at[1, :, y, c, :, mcol]

    def second_views(mid, fin, c0, w, half, pa):
        if mid is mid_g:
            col, both = pl.ds(c0, w), pl.ds(2 * half, 2)
            src = mid.at[half, :, pa, :, :, :, col]
            if half == 0:
                return src, fin.at[both, :, y, :, :, col]
            return src, fin.at[both, x, :, :, :, col]
        src = mid.at[half, pa, :, :, :, pl.ds(c0, w)]
        if half == 0:
            return src, fin.at[c0 // QUARTER, :, y]
        return src, fin.at[2 + c0 // QUARTER, x]

    def p1_copy(send, mid, st, c0, w, half, k):
        pc = lax.rem(c + lax.rem(k, 2), 2)
        pa = lax.rem((x if half == 0 else y) + k // 2, 4)
        peer = expert_id(pa, y, pc) if half == 0 else expert_id(x, pa, pc)
        src, dst = first_views(send, mid, c0, w, half, pa, pc)
        return pltpu.make_async_remote_copy(
            src_ref=src, dst_ref=dst, send_sem=p1_send.at[st, half], recv_sem=p1_recv.at[st, half],
            device_id=(z, peer), device_id_type=MESH,
        )

    def p1_self(send, mid, st, c0, w, half):
        src, dst = first_views(send, mid, c0, w, half, x if half == 0 else y, c)
        return pltpu.make_async_copy(src, dst, p1_recv.at[st, half])

    def p2_copy(mid, fin, st, c0, w, half, k):
        pa = lax.rem((y if half == 0 else x) + k, 4)
        peer = expert_id(x, pa, c) if half == 0 else expert_id(pa, y, c)
        src, dst = second_views(mid, fin, c0, w, half, pa)
        return pltpu.make_async_remote_copy(
            src_ref=src, dst_ref=dst, send_sem=p2_send.at[st, half], recv_sem=p2_recv.at[st, half],
            device_id=(z, peer), device_id_type=MESH,
        )

    def p2_self(mid, fin, st, c0, w, half):
        src, dst = second_views(mid, fin, c0, w, half, y if half == 0 else x)
        return pltpu.make_async_copy(src, dst, p2_recv.at[st, half])

    def each(lo, hi, fn):
        def step(k, _):
            fn(k)
            return 0

        lax.fori_loop(lo, hi, step, 0)

    def settle(view, sem):
        pltpu.make_async_copy(view, view, sem).wait()

    def share(w, blocks):
        return hid.at[0 : blocks * 128, :] if w == QUARTER else onehot.at[0 : blocks * 128, :]

    def start_first(args):
        send, mid, fin, st, c0, w = args

        def go(k):
            p1_copy(send, mid, st, c0, w, 0, k).start()
            p1_copy(send, mid, st, c0, w, 1, k).start()

        each(1, 8, go)
        for half in range(2):
            p1_self(send, mid, st, c0, w, half).start()

    def forward(args):
        send, mid, fin, st, c0, w = args
        for half in range(2):
            landed = mid.at[half, :, :, :, :, :, pl.ds(c0, w)] if mid is mid_g else mid.at[half, :, :, :, :, pl.ds(c0, w)]
            settle(landed, p1_recv.at[st, half])
            settle(share(w, 7), p1_send.at[st, half])
            each(1, 4, lambda k: p2_copy(mid, fin, st, c0, w, half, k).start())
            p2_self(mid, fin, st, c0, w, half).start()

    def arrive(args):
        send, mid, fin, st, c0, w = args
        for half in range(2):
            if mid is mid_g:
                landed = fin.at[pl.ds(2 * half, 2), :, :, :, :, pl.ds(c0, w)]
            else:
                landed = fin.at[2 * half + c0 // QUARTER]
            settle(landed, p2_recv.at[st, half])
            settle(share(w, 6), p2_send.at[st, half])

    wx, wg, wr = HALF // STAGES_X, QUARTER // STAGES_G, HALF // STAGES_R
    ex = [(send_x, mid_x, xs, s, s * wx, wx) for s in range(STAGES_X)]
    eg = [(send_g, mid_g, gs_, STAGES_X + s, s * wg, wg) for s in range(STAGES_G)]
    er = [(send_x, mid_x, send_g, STAGES_X + STAGES_G + s, s * wr, wr) for s in range(STAGES_R)]

    def activate(m):
        rows = jnp.concatenate([xs[b, m].reshape(256, QUARTER) for b in range(4)], axis=1)
        r = pl.ds(pl.multiple_of(m * 256, 256), 256)
        gate = dot(rows, win[0], 1, 0) * scale_in
        up = dot(rows, win[1], 1, 0) * scale_in
        sig = jax.nn.sigmoid(gate)
        act = gate * sig
        hid[r, :] = (act * up).astype(BF16)
        act_a[r, :] = up * sig * (1.0 + gate * (1.0 - sig))
        act_s[r, :] = act

    def out_copy(s, q):
        src = grad_s.at[2, q, :, pl.ds(s * wg, wg)]
        dst = grad_r.at[z, 2, :, pl.ds(s * wg, wg)]
        return pltpu.make_async_remote_copy(
            src_ref=src, dst_ref=dst, send_sem=rs_send.at[2], recv_sem=rs_recv.at[2],
            device_id=(q, e), device_id_type=MESH,
        ), pltpu.make_async_copy(src, dst, rs_recv.at[2])

    def grad_out(s):
        cols = slice(s * wg, s * wg + wg)
        rows = jnp.concatenate([gs_[q, :, :, :, :, cols].reshape(ROWS, wg) for q in range(4)], axis=1)
        out = (dot(hid[...], rows, 0, 0) * scale_out).astype(BF16)
        for q in range(4):
            grad_s[2, q, :, cols] = out[:, q * wg : (q + 1) * wg]
            remote, local = out_copy(s, q)

            @pl.when(z != q)
            def _():
                remote.start()

            @pl.when(z == q)
            def _():
                local.start()

    def hidden_grad(s):
        def step(m, _):
            r = pl.ds(pl.multiple_of(m * 256, 256), 256)
            cols = slice(s * wg, s * wg + wg)
            rows = jnp.concatenate([gs_[q, m, :, :, :, cols].reshape(256, wg) for q in range(4)], axis=1)
            down = jnp.concatenate(
                [wout[:, q * QUARTER + s * wg : q * QUARTER + s * wg + wg] for q in range(4)], axis=1
            )
            acc = dot(rows, down, 1, 1)
            if s > 0:
                acc = acc + dh[r, :]
            if s < STAGES_G - 1:
                dh[r, :] = acc
            else:
                acc = acc * scale_out
                dgu[0, r, :] = (acc * act_a[r, :]).astype(BF16)
                dgu[1, r, :] = (acc * act_s[r, :]).astype(BF16)
            return 0

        lax.fori_loop(0, 4, step, 0)

    def in_copy(mat, k):
        q = lax.rem(z + k, 4)
        return pltpu.make_async_remote_copy(
            src_ref=grad_s.at[mat, q], dst_ref=grad_r.at[z, mat],
            send_sem=rs_send.at[mat], recv_sem=rs_recv.at[mat],
            device_id=(q, e), device_id_type=MESH,
        )

    def in_self(mat):
        return pltpu.make_async_copy(grad_s.at[mat, z], grad_r.at[z, mat], rs_recv.at[mat])

    def grad_in(mat):
        def step(j, _):
            k = lax.rem(2 + 3 * j, 4)
            q = lax.rem(z + k, 4)
            rows = xs[q].reshape(ROWS, QUARTER)
            grad_s[mat, q] = (dot(rows, dgu[mat], 0, 0) * scale_in).astype(BF16)

            @pl.when(k != 0)
            def _():
                in_copy(mat, k).start()

            @pl.when(k == 0)
            def _():
                in_self(mat).start()

            return 0

        lax.fori_loop(0, 4, step, 0)

    def rows_back(s):
        def step(m, _):
            r = pl.ds(pl.multiple_of(m * 256, 256), 256)
            for half in range(2):
                col = half * HALF + s * wr
                v = dot(dgu[0, r, :], win[0, col : col + wr, :], 1, 1)
                v = v + dot(dgu[1, r, :], win[1, col : col + wr, :], 1, 1)
                send_x[m, :, :, :, col : col + wr] = (v * scale_in).astype(BF16).reshape(4, 2, CAP, wr)
            return 0

        lax.fori_loop(0, 4, step, 0)

    pairs = [(0, 0), (1, 1), (2, 2), (3, 3), (0, 1), (0, 2), (0, 3), (1, 2), (1, 3), (2, 3)]

    def fold(v):
        total = None
        for i in range(v.shape[0] // 8):
            for j in range(v.shape[1] // 128):
                part = v[i * 8 : (i + 1) * 8, j * 128 : (j + 1) * 128]
                total = part if total is None else total + part
        return total

    def gram_of(mat, sums):
        def step(i, sums):
            r = pl.ds(pl.multiple_of(i * 16, 16), 16)
            g = [grad_r[s, mat, r, :].astype(F32) for s in range(4)]
            return tuple(t + fold(g[a] * g[b]) for t, (a, b) in zip(sums, pairs))

        return lax.fori_loop(0, 32, step, sums)

    load[0].wait()
    gather(tok, send_x, ex[0][4], wx, False)
    pl.semaphore_wait(barrier, 16)
    start_first(ex[0])
    for copy in load[2:]:
        copy.start()
    gather(tok, send_x, ex[1][4], wx, False)
    start_first(ex[1])
    load[1].wait()
    gather(cot, send_g, eg[0][4], wg, True)
    gather(cot, send_g, eg[1][4], wg, True)
    forward(ex[0])
    start_first(eg[0])
    gather(cot, send_g, eg[2][4], wg, True)
    gather(cot, send_g, eg[3][4], wg, True)
    forward(ex[1])
    start_first(eg[1])
    forward(eg[0])
    start_first(eg[2])
    load[2].wait()
    load[3].wait()
    arrive(ex[0])
    arrive(ex[1])
    start_first(eg[3])
    each(0, 2, activate)
    forward(eg[1])
    each(2, 4, activate)
    forward(eg[2])
    arrive(eg[0])
    grad_out(0)
    hidden_grad(0)
    arrive(eg[1])
    grad_out(1)
    hidden_grad(1)
    forward(eg[3])
    arrive(eg[2])
    grad_out(2)
    hidden_grad(2)
    arrive(eg[3])
    grad_out(3)
    hidden_grad(3)
    grad_in(0)
    grad_in(1)
    for s in range(STAGES_R):
        rows_back(s)
        start_first(er[s])

    sums = tuple(jnp.zeros((8, 128), F32) for _ in pairs)
    settle(grad_r.at[:, 2], rs_recv.at[2])
    settle(grad_s.at[2, 0:3], rs_send.at[2])
    sums = gram_of(2, sums)
    for s in range(STAGES_R):
        forward(er[s])
    for mat in range(2):
        settle(grad_r.at[:, mat], rs_recv.at[mat])
        settle(grad_s.at[mat, 0:3], rs_send.at[mat])
        sums = gram_of(mat, sums)

    own = jnp.concatenate([jnp.sum(t, axis=0, keepdims=True) for t in sums] + [jnp.zeros((6, 128), F32)], axis=0)
    gram[z] = own

    def gram_copy(k):
        return pltpu.make_async_remote_copy(
            src_ref=gram.at[z], dst_ref=gram.at[z], send_sem=gram_sem.at[0], recv_sem=gram_sem.at[1],
            device_id=(lax.rem(z + k, 4), e), device_id_type=MESH,
        )

    each(1, 4, lambda k: gram_copy(k).start())
    load[4].wait()
    load[5].wait()
    settle(gram.at[0:3], gram_sem.at[1])
    settle(gram.at[0:3], gram_sem.at[0])
    total = jnp.sum(gram[0] + gram[1] + gram[2] + gram[3], axis=1, keepdims=True)
    dots = {p: total[i : i + 1, :] for i, p in enumerate(pairs)}

    def coefficient(cross, norm):
        return 1.0 - cross / (2.0 * (norm + EPS))

    a0 = coefficient(dots[0, 2], dots[0, 0])
    a2 = coefficient(dots[0, 2], dots[2, 2])
    a1 = coefficient(dots[1, 3], dots[1, 1])
    a3 = coefficient(dots[1, 3], dots[3, 3])
    n0 = a0 * a0 * dots[0, 0] + 2.0 * a0 * a2 * dots[0, 2] + a2 * a2 * dots[2, 2]
    n1 = a1 * a1 * dots[1, 1] + 2.0 * a1 * a3 * dots[1, 3] + a3 * a3 * dots[3, 3]
    cross = a0 * (a1 * dots[0, 1] + a3 * dots[0, 3]) + a2 * (a1 * dots[1, 2] + a3 * dots[2, 3])
    b0 = coefficient(cross, jnp.maximum(n0, 0.0))
    b1 = coefficient(cross, jnp.maximum(n1, 0.0))
    coef = [b0 * a0, b1 * a1, b0 * a2, b1 * a3]

    def slot(mat, hh, owner):
        if mat < 2:
            return xs.at[2 * mat + owner // 2, 2 * lax.rem(owner, 2) + hh]
        return nwout.at[pl.ds(hh * 256, 256), pl.ds(pl.multiple_of(owner * QUARTER, QUARTER), QUARTER)]

    def ag_copy(mat, hh, direction):
        return pltpu.make_async_remote_copy(
            src_ref=slot(mat, hh, z), dst_ref=slot(mat, hh, z),
            send_sem=ag_send.at[0], recv_sem=ag_recv.at[2 * mat + hh] if direction == hh else ag_last.at[0],
            device_id=(lax.rem(z + (1 if direction == 0 else 3), 4), e), device_id_type=MESH,
        )

    def fw_copy(mat, hh):
        owner = lax.rem(z + (3 if hh == 0 else 1), 4)
        return pltpu.make_async_remote_copy(
            src_ref=slot(mat, hh, owner), dst_ref=slot(mat, hh, owner),
            send_sem=fw_sem.at[0], recv_sem=fw_sem.at[1],
            device_id=(lax.rem(z + (1 if hh == 0 else 3), 4), e), device_id_type=MESH,
        )

    for mat in range(3):
        for hh in range(2):

            def step(i, _):
                r = pl.multiple_of(hh * 256 + i * 32, 32)
                rr = pl.ds(r, 32)
                comb = coef[0] * grad_r[0, mat, rr, :].astype(F32)
                for s in range(1, 4):
                    comb = comb + coef[s] * grad_r[s, mat, rr, :].astype(F32)
                if mat < 2:
                    new = MOMENTUM * mom_in[mat, rr, :] + comb
                    mom_in[mat, rr, :] = new
                    old = win[mat, pl.ds(pl.multiple_of(z * QUARTER + r, 32), 32), :]
                else:
                    new = MOMENTUM * mom_out[rr, :] + comb
                    mom_out[rr, :] = new
                    old = wout[rr, pl.ds(pl.multiple_of(z * QUARTER, QUARTER), QUARTER)]
                value = (old.astype(F32) - RATE * new).astype(BF16)
                if mat < 2:
                    xs[2 * mat + z // 2, 2 * lax.rem(z, 2) + hh, i // 2, lax.rem(i, 2)] = value
                else:
                    nwout[rr, pl.ds(pl.multiple_of(z * QUARTER, QUARTER), QUARTER)] = value
                return 0

            lax.fori_loop(0, 8, step, 0)
            ag_copy(mat, hh, 0).start()
            ag_copy(mat, hh, 1).start()

    def pass_on(mat, hh):
        ag_copy(mat, hh, hh).wait_recv()
        fw_copy(mat, hh).start()

    pass_on(0, 0)
    pass_on(0, 1)

    for s in range(STAGES_R):
        arrive(er[s])

    def tokens_step(n, _):
        cols = pl.ds(pl.multiple_of(n * 512, 512), 512)
        rows = send_g[n].reshape(ROWS, 512)
        tok[:, cols] = dot(onehot[...], rows, 0, 0).astype(BF16)
        return 0

    lax.fori_loop(0, 4, tokens_step, 0)

    for mat in range(1, 3):
        for hh in range(2):
            pass_on(mat, hh)
    settle(grad_s.at[0, 0:3], ag_last.at[0])
    settle(grad_s.at[0:3, 0:2], ag_send.at[0])
    settle(grad_s.at[0, 0:3], fw_sem.at[0])
    settle(grad_s.at[0, 0:3], fw_sem.at[1])


def write_out(*refs):
    sources, targets, sem = refs[:5], refs[5:10], refs[10]
    copies = []
    for source, target in zip(sources, targets):
        parts = source.shape[0] if len(source.shape) != 2 else 2
        rows = source.shape[0] // parts
        for part in range(parts):
            at = pl.ds(part * rows, rows)
            copies.append(pltpu.make_async_copy(source.at[at], target.at[at], sem.at[len(copies)]))
    for copy in copies:
        copy.start()
    for copy in copies:
        copy.wait()


def shards(tokens, cotangent, slot_rows, slot_count, slot_weight, w_in, w_out, momentum_in, momentum_out):
    any_ = pl.BlockSpec(memory_space=pl.ANY)
    vmem = pl.BlockSpec(memory_space=pltpu.VMEM)
    stages = STAGES_X + STAGES_G + STAGES_R
    grid5 = (4, 4, 2, CAP, D)
    mid = (2, 4, 4, 2, CAP, HALF)
    blocks = (4, 4, 4, 2, CAP, QUARTER)
    mid_blocks = (2, 2, 4, 4, 2, CAP, QUARTER)
    dma = pltpu.SemaphoreType.DMA
    outs = pl.pallas_call(
        kernel,
        out_shape=(
            pltpu.VMEM((256, D), BF16),
            pltpu.VMEM(blocks, BF16),
            pltpu.VMEM((FF, D), BF16),
            pltpu.VMEM((2, QUARTER, FF), F32),
            pltpu.VMEM((FF, QUARTER), F32),
        ),
        in_specs=[any_, any_, vmem, vmem, vmem, any_, any_, any_, any_],
        out_specs=(vmem,) * 5,
        scratch_shapes=[
            pltpu.VMEM((256, D), BF16),
            pltpu.VMEM((ROWS, 256), BF16),
            pltpu.VMEM((ROWS, 128), F32),
            pltpu.VMEM(grid5, BF16),
            pltpu.VMEM(blocks, BF16),
            pltpu.VMEM(mid, BF16),
            pltpu.VMEM(mid_blocks, BF16),
            pltpu.VMEM(blocks, BF16),
            pltpu.VMEM((2, D, FF), BF16),
            pltpu.VMEM((FF, D), BF16),
            pltpu.VMEM((ROWS, FF), F32),
            pltpu.VMEM((ROWS, FF), F32),
            pltpu.VMEM((ROWS, FF), BF16),
            pltpu.VMEM((ROWS, FF), F32),
            pltpu.VMEM((2, ROWS, FF), BF16),
            pltpu.VMEM((3, 4, QUARTER, QUARTER), BF16),
            pltpu.VMEM((4, 3, QUARTER, QUARTER), BF16),
            pltpu.VMEM((4, 16, 128), F32),
            dma((6,)),
            dma((stages, 2)),
            dma((stages, 2)),
            dma((stages, 2)),
            dma((stages, 2)),
            dma((3,)),
            dma((3,)),
            dma((2,)),
            dma((1,)),
            dma((6,)),
            dma((1,)),
            dma((2,)),
        ],
        compiler_params=pltpu.CompilerParams(
            collective_id=0, has_side_effects=True, vmem_limit_bytes=53 << 20
        ),
        name="step",
    )(
        tokens[0], cotangent[0], slot_rows[0, 0], slot_count[0], slot_weight[0, 0],
        w_in[0], w_out[0], momentum_in[0], momentum_out[0],
    )
    outs = [pltpu.with_memory_space_constraint(o, pltpu.VMEM) for o in outs]
    outs = pl.pallas_call(
        write_out,
        out_shape=[pltpu.HBM(o.shape, o.dtype) for o in outs],
        in_specs=[vmem] * 5,
        out_specs=[pl.BlockSpec(memory_space=pltpu.HBM)] * 5,
        scratch_shapes=[dma((16,))],
        compiler_params=pltpu.CompilerParams(vmem_limit_bytes=1 << 20),
        name="write_out",
    )(*outs)
    outs = (outs[0], outs[1].reshape(2, D, FF)) + tuple(outs[2:])
    return tuple(o[None] for o in outs)


def solution(mesh):
    return jax.shard_map(
        shards,
        mesh=mesh,
        in_specs=(
            P("dp", "expert", None),
            P("dp", "expert", None),
            P("dp", "expert", None, None),
            P("dp", "expert", None),
            P("dp", "expert", None, None),
            P("expert", None, None, None),
            P("expert", None, None),
            P("expert", None, "dp", None),
            P("expert", None, "dp"),
        ),
        out_specs=(
            P("dp", "expert", None),
            P("expert", None, None, None),
            P("expert", None, None),
            P("expert", None, "dp", None),
            P("expert", None, "dp"),
        ),
        check_vma=False,
    )
```

```python
import jax
import jax.numpy as jnp
from jax import lax
from jax.experimental import pallas as pl
from jax.experimental.pallas import tpu as pltpu
from jax.sharding import PartitionSpec as P

EPS = 1e-06
MOMENTUM = 0.9
RATE = 0.1
MESH = pl.DeviceIdType.MESH

D = 2048
FF = 512
HALF = 1024
QUARTER = 512
CAP = 32
STAGES_X = 2
STAGES_G = 4
STAGES_R = 2
ROWS = 1024
BF16 = jnp.bfloat16
F32 = jnp.float32


def dot(a, b, ca, cb):
    return lax.dot_general(a, b, (((ca,), (cb,)), ((), ())), preferred_element_type=F32)


def kernel(
    tok_h, cot_h, rows_v, count_v, weight_v, win_h, wout_h, min_h, mout_h,
    tok, xs, nwout, mom_in, mom_out,
    cot, onehot, scale, send_x, send_g, mid_x, mid_g, gs_, win, wout,
    act_a, act_s, hid, dh, dgu, grad_s, grad_r, gram,
    load_sem, p1_send, p1_recv, p2_send, p2_recv,
    rs_send, rs_recv, gram_sem, ag_send, ag_recv, ag_last, fw_sem,
):
    z = lax.axis_index("dp")
    e = lax.axis_index("expert")
    x = e // 8
    y = lax.rem(e // 2, 4)
    c = lax.rem(e, 2)
    scale_in = D ** (-0.5)
    scale_out = FF ** (-0.5)

    def expert_id(px, py, pc):
        return (px * 4 + py) * 2 + pc

    loads = [
        (tok_h, tok), (cot_h, cot), (win_h, win), (wout_h, wout), (min_h, mom_in), (mout_h, mom_out),
    ]
    load = [pltpu.make_async_copy(s, d, load_sem.at[i]) for i, (s, d) in enumerate(loads)]
    for copy in load[:2]:
        copy.start()

    barrier = pltpu.get_barrier_semaphore()

    def greet(device):
        pl.semaphore_signal(barrier, inc=1, device_id=device, device_id_type=MESH)

    for k in range(1, 8):
        greet((z, expert_id(lax.rem(x + k // 2, 4), y, lax.rem(c + k % 2, 2))))
    for k in range(2, 8):
        greet((z, expert_id(x, lax.rem(y + k // 2, 4), lax.rem(c + k % 2, 2))))
    for k in range(1, 4):
        greet((lax.rem(z + k, 4), e))

    rows_t = jnp.transpose(rows_v[...])
    weight_t = jnp.transpose(weight_v[...])
    valid = lax.broadcasted_iota(jnp.int32, (CAP, 32), 0) < count_v[...]
    scale_t = jnp.where(valid, weight_t, 0.0)
    lane = lax.broadcasted_iota(jnp.int32, (CAP, 256), 1)
    for k in range(32):
        onehot[k * CAP : (k + 1) * CAP, :] = (lane == rows_t[:, k : k + 1]).astype(F32).astype(BF16)
        scale[k * CAP : (k + 1) * CAP, :] = jnp.broadcast_to(scale_t[:, k : k + 1], (CAP, 128))

    def gather(src, dst, c0, w, scaled):
        def step(m, _):
            r0 = pl.multiple_of(m * 256, 256)
            hot = onehot[pl.ds(r0, 256), :]
            if scaled:
                for q in range(4):
                    v = dot(hot, src[:, q * QUARTER + c0 : q * QUARTER + c0 + w], 1, 0)
                    v = v * scale[pl.ds(r0, 256), 0:1]
                    dst[q, m, :, :, :, c0 : c0 + w] = v.astype(BF16).reshape(4, 2, CAP, w)
            else:
                for half in range(2):
                    col = half * HALF + c0
                    v = dot(hot, src[:, col : col + w], 1, 0)
                    dst[m, :, :, :, col : col + w] = v.astype(BF16).reshape(4, 2, CAP, w)
            return 0

        lax.fori_loop(0, 4, step, 0)

    def first_views(send, mid, c0, w, half, pa, pc):
        if send is send_g:
            col, both = pl.ds(c0, w), pl.ds(2 * half, 2)
            if half == 0:
                return send.at[both, pa, :, pc, :, col], mid.at[0, :, :, x, c, :, col]
            return send.at[both, :, pa, pc, :, col], mid.at[1, :, :, y, c, :, col]
        col, mcol = pl.ds(half * HALF + c0, w), pl.ds(c0, w)
        if half == 0:
            return send.at[pa, :, pc, :, col], mid.at[0, :, x, c, :, mcol]
        return send.at[:, pa, pc, :, col], mid.at[1, :, y, c, :, mcol]

    def second_views(mid, fin, c0, w, half, pa):
        if mid is mid_g:
            col, both = pl.ds(c0, w), pl.ds(2 * half, 2)
            src = mid.at[half, :, pa, :, :, :, col]
            if half == 0:
                return src, fin.at[both, :, y, :, :, col]
            return src, fin.at[both, x, :, :, :, col]
        src = mid.at[half, pa, :, :, :, pl.ds(c0, w)]
        if half == 0:
            return src, fin.at[c0 // QUARTER, :, y]
        return src, fin.at[2 + c0 // QUARTER, x]

    def p1_copy(send, mid, st, c0, w, half, k):
        pc = lax.rem(c + lax.rem(k, 2), 2)
        pa = lax.rem((x if half == 0 else y) + k // 2, 4)
        peer = expert_id(pa, y, pc) if half == 0 else expert_id(x, pa, pc)
        src, dst = first_views(send, mid, c0, w, half, pa, pc)
        return pltpu.make_async_remote_copy(
            src_ref=src, dst_ref=dst, send_sem=p1_send.at[st, half], recv_sem=p1_recv.at[st, half],
            device_id=(z, peer), device_id_type=MESH,
        )

    def p1_self(send, mid, st, c0, w, half):
        src, dst = first_views(send, mid, c0, w, half, x if half == 0 else y, c)
        return pltpu.make_async_copy(src, dst, p1_recv.at[st, half])

    def p2_copy(mid, fin, st, c0, w, half, k):
        pa = lax.rem((y if half == 0 else x) + k, 4)
        peer = expert_id(x, pa, c) if half == 0 else expert_id(pa, y, c)
        src, dst = second_views(mid, fin, c0, w, half, pa)
        return pltpu.make_async_remote_copy(
            src_ref=src, dst_ref=dst, send_sem=p2_send.at[st, half], recv_sem=p2_recv.at[st, half],
            device_id=(z, peer), device_id_type=MESH,
        )

    def p2_self(mid, fin, st, c0, w, half):
        src, dst = second_views(mid, fin, c0, w, half, y if half == 0 else x)
        return pltpu.make_async_copy(src, dst, p2_recv.at[st, half])

    def each(lo, hi, fn):
        def step(k, _):
            fn(k)
            return 0

        lax.fori_loop(lo, hi, step, 0)

    def settle(view, sem):
        pltpu.make_async_copy(view, view, sem).wait()

    def share(w, blocks):
        return hid.at[0 : blocks * 128, :] if w == QUARTER else onehot.at[0 : blocks * 128, :]

    def start_first(args):
        send, mid, fin, st, c0, w = args

        def go(k):
            p1_copy(send, mid, st, c0, w, 0, k).start()
            p1_copy(send, mid, st, c0, w, 1, k).start()

        each(1, 8, go)
        for half in range(2):
            p1_self(send, mid, st, c0, w, half).start()

    def forward(args):
        send, mid, fin, st, c0, w = args
        for half in range(2):
            landed = mid.at[half, :, :, :, :, :, pl.ds(c0, w)] if mid is mid_g else mid.at[half, :, :, :, :, pl.ds(c0, w)]
            settle(landed, p1_recv.at[st, half])
            settle(share(w, 7), p1_send.at[st, half])
            each(1, 4, lambda k: p2_copy(mid, fin, st, c0, w, half, k).start())
            p2_self(mid, fin, st, c0, w, half).start()

    def arrive(args):
        send, mid, fin, st, c0, w = args
        for half in range(2):
            if mid is mid_g:
                landed = fin.at[pl.ds(2 * half, 2), :, :, :, :, pl.ds(c0, w)]
            else:
                landed = fin.at[2 * half + c0 // QUARTER]
            settle(landed, p2_recv.at[st, half])
            settle(share(w, 6), p2_send.at[st, half])

    wx, wg, wr = HALF // STAGES_X, QUARTER // STAGES_G, HALF // STAGES_R
    ex = [(send_x, mid_x, xs, s, s * wx, wx) for s in range(STAGES_X)]
    eg = [(send_g, mid_g, gs_, STAGES_X + s, s * wg, wg) for s in range(STAGES_G)]
    er = [(send_x, mid_x, send_g, STAGES_X + STAGES_G + s, s * wr, wr) for s in range(STAGES_R)]

    def activate(m):
        rows = jnp.concatenate([xs[b, m].reshape(256, QUARTER) for b in range(4)], axis=1)
        r = pl.ds(pl.multiple_of(m * 256, 256), 256)
        gate = dot(rows, win[0], 1, 0) * scale_in
        up = dot(rows, win[1], 1, 0) * scale_in
        sig = jax.nn.sigmoid(gate)
        act = gate * sig
        hid[r, :] = (act * up).astype(BF16)
        act_a[r, :] = up * sig * (1.0 + gate * (1.0 - sig))
        act_s[r, :] = act

    def out_copy(s, q):
        src = grad_s.at[2, q, :, pl.ds(s * wg, wg)]
        dst = grad_r.at[z, 2, :, pl.ds(s * wg, wg)]
        return pltpu.make_async_remote_copy(
            src_ref=src, dst_ref=dst, send_sem=rs_send.at[2], recv_sem=rs_recv.at[4],
            device_id=(q, e), device_id_type=MESH,
        ), pltpu.make_async_copy(src, dst, rs_recv.at[4])

    def grad_out(s):
        cols = slice(s * wg, s * wg + wg)
        rows = jnp.concatenate([gs_[q, :, :, :, :, cols].reshape(ROWS, wg) for q in range(4)], axis=1)
        out = (dot(hid[...], rows, 0, 0) * scale_out).astype(BF16)
        for q in range(4):
            grad_s[2, q, :, cols] = out[:, q * wg : (q + 1) * wg]
            remote, local = out_copy(s, q)

            @pl.when(z != q)
            def _():
                remote.start()

            @pl.when(z == q)
            def _():
                local.start()

    def hidden_grad(s):
        def step(m, _):
            r = pl.ds(pl.multiple_of(m * 256, 256), 256)
            cols = slice(s * wg, s * wg + wg)
            rows = jnp.concatenate([gs_[q, m, :, :, :, cols].reshape(256, wg) for q in range(4)], axis=1)
            down = jnp.concatenate(
                [wout[:, q * QUARTER + s * wg : q * QUARTER + s * wg + wg] for q in range(4)], axis=1
            )
            acc = dot(rows, down, 1, 1)
            if s > 0:
                acc = acc + dh[r, :]
            if s < STAGES_G - 1:
                dh[r, :] = acc
            else:
                acc = acc * scale_out
                dgu[0, r, :] = (acc * act_a[r, :]).astype(BF16)
                dgu[1, r, :] = (acc * act_s[r, :]).astype(BF16)
            return 0

        lax.fori_loop(0, 4, step, 0)

    def in_copy(mat, hh, k):
        q = lax.rem(z + k, 4)
        part = pl.ds(hh * 256, 256)
        return pltpu.make_async_remote_copy(
            src_ref=grad_s.at[mat, q, part], dst_ref=grad_r.at[z, mat, part],
            send_sem=rs_send.at[mat], recv_sem=rs_recv.at[2 * mat + hh],
            device_id=(q, e), device_id_type=MESH,
        )

    def in_self(mat, hh):
        part = pl.ds(hh * 256, 256)
        return pltpu.make_async_copy(
            grad_s.at[mat, z, part], grad_r.at[z, mat, part], rs_recv.at[2 * mat + hh]
        )

    def grad_in(mat, hh):
        def step(j, _):
            k = lax.rem(1 + 2 * j + j // 2, 4)
            q = lax.rem(z + k, 4)
            rows = xs[q, :, :, :, :, hh * 256 : hh * 256 + 256].reshape(ROWS, 256)
            grad_s[mat, q, hh * 256 : hh * 256 + 256] = (dot(rows, dgu[mat], 0, 0) * scale_in).astype(BF16)

            @pl.when(k != 0)
            def _():
                in_copy(mat, hh, k).start()

            @pl.when(k == 0)
            def _():
                in_self(mat, hh).start()

            return 0

        lax.fori_loop(0, 4, step, 0)

    def rows_back(s):
        def step(m, _):
            r = pl.ds(pl.multiple_of(m * 256, 256), 256)
            for half in range(2):
                col = half * HALF + s * wr
                v = dot(dgu[0, r, :], win[0, col : col + wr, :], 1, 1)
                v = v + dot(dgu[1, r, :], win[1, col : col + wr, :], 1, 1)
                send_x[m, :, :, :, col : col + wr] = (v * scale_in).astype(BF16).reshape(4, 2, CAP, wr)
            return 0

        lax.fori_loop(0, 4, step, 0)

    pairs = [(0, 0), (1, 1), (2, 2), (3, 3), (0, 1), (0, 2), (0, 3), (1, 2), (1, 3), (2, 3)]

    def fold(v):
        total = None
        for i in range(v.shape[0] // 8):
            for j in range(v.shape[1] // 128):
                part = v[i * 8 : (i + 1) * 8, j * 128 : (j + 1) * 128]
                total = part if total is None else total + part
        return total

    def gram_of(mat, hh, sums):
        def step(i, sums):
            r = pl.ds(pl.multiple_of(hh * 256 + i * 16, 16), 16)
            g = [grad_r[s, mat, r, :].astype(F32) for s in range(4)]
            return tuple(t + fold(g[a] * g[b]) for t, (a, b) in zip(sums, pairs))

        return lax.fori_loop(0, 16, step, sums)

    load[0].wait()
    gather(tok, send_x, ex[0][4], wx, False)
    pl.semaphore_wait(barrier, 16)
    start_first(ex[0])
    for copy in load[2:]:
        copy.start()
    gather(tok, send_x, ex[1][4], wx, False)
    start_first(ex[1])
    load[1].wait()
    gather(cot, send_g, eg[0][4], wg, True)
    gather(cot, send_g, eg[1][4], wg, True)
    forward(ex[0])
    start_first(eg[0])
    gather(cot, send_g, eg[2][4], wg, True)
    gather(cot, send_g, eg[3][4], wg, True)
    forward(ex[1])
    start_first(eg[1])
    forward(eg[0])
    start_first(eg[2])
    load[2].wait()
    load[3].wait()
    arrive(ex[0])
    arrive(ex[1])
    start_first(eg[3])
    each(0, 2, activate)
    forward(eg[1])
    each(2, 4, activate)
    forward(eg[2])
    arrive(eg[0])
    grad_out(0)
    hidden_grad(0)
    forward(eg[3])
    arrive(eg[1])
    grad_out(1)
    hidden_grad(1)
    arrive(eg[2])
    grad_out(2)
    hidden_grad(2)
    arrive(eg[3])
    grad_out(3)
    hidden_grad(3)
    for mat in range(2):
        for hh in range(2):
            grad_in(mat, hh)
    for s in range(STAGES_R):
        rows_back(s)
        start_first(er[s])

    sums = tuple(jnp.zeros((8, 128), F32) for _ in pairs)
    settle(grad_r.at[:, 2], rs_recv.at[4])
    settle(grad_s.at[2, 0:3], rs_send.at[2])
    sums = gram_of(2, 1, gram_of(2, 0, sums))
    for s in range(STAGES_R):
        forward(er[s])
    for mat in range(2):
        for hh in range(2):
            settle(grad_r.at[:, mat, pl.ds(hh * 256, 256)], rs_recv.at[2 * mat + hh])
            sums = gram_of(mat, hh, sums)
        settle(grad_s.at[mat, 0:3], rs_send.at[mat])

    own = jnp.concatenate([jnp.sum(t, axis=0, keepdims=True) for t in sums] + [jnp.zeros((6, 128), F32)], axis=0)
    gram[z] = own

    def gram_copy(k):
        return pltpu.make_async_remote_copy(
            src_ref=gram.at[z], dst_ref=gram.at[z], send_sem=gram_sem.at[0], recv_sem=gram_sem.at[1],
            device_id=(lax.rem(z + k, 4), e), device_id_type=MESH,
        )

    each(1, 4, lambda k: gram_copy(k).start())
    load[4].wait()
    load[5].wait()
    settle(gram.at[0:3], gram_sem.at[1])
    settle(gram.at[0:3], gram_sem.at[0])
    total = jnp.sum(gram[0] + gram[1] + gram[2] + gram[3], axis=1, keepdims=True)
    dots = {p: total[i : i + 1, :] for i, p in enumerate(pairs)}

    def coefficient(cross, norm):
        return 1.0 - cross / (2.0 * (norm + EPS))

    a0 = coefficient(dots[0, 2], dots[0, 0])
    a2 = coefficient(dots[0, 2], dots[2, 2])
    a1 = coefficient(dots[1, 3], dots[1, 1])
    a3 = coefficient(dots[1, 3], dots[3, 3])
    n0 = a0 * a0 * dots[0, 0] + 2.0 * a0 * a2 * dots[0, 2] + a2 * a2 * dots[2, 2]
    n1 = a1 * a1 * dots[1, 1] + 2.0 * a1 * a3 * dots[1, 3] + a3 * a3 * dots[3, 3]
    cross = a0 * (a1 * dots[0, 1] + a3 * dots[0, 3]) + a2 * (a1 * dots[1, 2] + a3 * dots[2, 3])
    b0 = coefficient(cross, jnp.maximum(n0, 0.0))
    b1 = coefficient(cross, jnp.maximum(n1, 0.0))
    coef = [b0 * a0, b1 * a1, b0 * a2, b1 * a3]

    def slot(mat, hh, owner):
        if mat < 2:
            return xs.at[2 * mat + owner // 2, 2 * lax.rem(owner, 2) + hh]
        return nwout.at[pl.ds(hh * 256, 256), pl.ds(pl.multiple_of(owner * QUARTER, QUARTER), QUARTER)]

    def ag_copy(mat, hh, direction):
        return pltpu.make_async_remote_copy(
            src_ref=slot(mat, hh, z), dst_ref=slot(mat, hh, z),
            send_sem=ag_send.at[0], recv_sem=ag_recv.at[2 * mat + hh] if direction == hh else ag_last.at[0],
            device_id=(lax.rem(z + (1 if direction == 0 else 3), 4), e), device_id_type=MESH,
        )

    def fw_copy(mat, hh):
        owner = lax.rem(z + (3 if hh == 0 else 1), 4)
        return pltpu.make_async_remote_copy(
            src_ref=slot(mat, hh, owner), dst_ref=slot(mat, hh, owner),
            send_sem=fw_sem.at[0], recv_sem=fw_sem.at[1],
            device_id=(lax.rem(z + (1 if hh == 0 else 3), 4), e), device_id_type=MESH,
        )

    for mat in range(3):
        for hh in range(2):

            def step(i, _):
                r = pl.multiple_of(hh * 256 + i * 32, 32)
                rr = pl.ds(r, 32)
                comb = coef[0] * grad_r[0, mat, rr, :].astype(F32)
                for s in range(1, 4):
                    comb = comb + coef[s] * grad_r[s, mat, rr, :].astype(F32)
                if mat < 2:
                    new = MOMENTUM * mom_in[mat, rr, :] + comb
                    mom_in[mat, rr, :] = new
                    old = win[mat, pl.ds(pl.multiple_of(z * QUARTER + r, 32), 32), :]
                else:
                    new = MOMENTUM * mom_out[rr, :] + comb
                    mom_out[rr, :] = new
                    old = wout[rr, pl.ds(pl.multiple_of(z * QUARTER, QUARTER), QUARTER)]
                value = (old.astype(F32) - RATE * new).astype(BF16)
                if mat < 2:
                    xs[2 * mat + z // 2, 2 * lax.rem(z, 2) + hh, i // 2, lax.rem(i, 2)] = value
                else:
                    nwout[rr, pl.ds(pl.multiple_of(z * QUARTER, QUARTER), QUARTER)] = value
                return 0

            lax.fori_loop(0, 8, step, 0)
            ag_copy(mat, hh, 0).start()
            ag_copy(mat, hh, 1).start()

    def pass_on(mat, hh):
        ag_copy(mat, hh, hh).wait_recv()
        fw_copy(mat, hh).start()

    pass_on(0, 0)
    pass_on(0, 1)

    for s in range(STAGES_R):
        arrive(er[s])

    def tokens_step(n, _):
        cols = pl.ds(pl.multiple_of(n * 512, 512), 512)
        rows = send_g[n].reshape(ROWS, 512)
        tok[:, cols] = dot(onehot[...], rows, 0, 0).astype(BF16)
        return 0

    lax.fori_loop(0, 4, tokens_step, 0)

    for mat in range(1, 3):
        for hh in range(2):
            pass_on(mat, hh)
    settle(grad_s.at[0, 0:3], ag_last.at[0])
    settle(grad_s.at[0:3, 0:2], ag_send.at[0])
    settle(grad_s.at[0, 0:3], fw_sem.at[0])
    settle(grad_s.at[0, 0:3], fw_sem.at[1])


def write_out(*refs):
    sources, targets, sem = refs[:5], refs[5:10], refs[10]
    copies = []
    for source, target in zip(sources, targets):
        parts = source.shape[0] if len(source.shape) != 2 else 2
        rows = source.shape[0] // parts
        for part in range(parts):
            at = pl.ds(part * rows, rows)
            copies.append(pltpu.make_async_copy(source.at[at], target.at[at], sem.at[len(copies)]))
    for copy in copies:
        copy.start()
    for copy in copies:
        copy.wait()


def shards(tokens, cotangent, slot_rows, slot_count, slot_weight, w_in, w_out, momentum_in, momentum_out):
    any_ = pl.BlockSpec(memory_space=pl.ANY)
    vmem = pl.BlockSpec(memory_space=pltpu.VMEM)
    stages = STAGES_X + STAGES_G + STAGES_R
    grid5 = (4, 4, 2, CAP, D)
    mid = (2, 4, 4, 2, CAP, HALF)
    blocks = (4, 4, 4, 2, CAP, QUARTER)
    mid_blocks = (2, 2, 4, 4, 2, CAP, QUARTER)
    dma = pltpu.SemaphoreType.DMA
    outs = pl.pallas_call(
        kernel,
        out_shape=(
            pltpu.VMEM((256, D), BF16),
            pltpu.VMEM(blocks, BF16),
            pltpu.VMEM((FF, D), BF16),
            pltpu.VMEM((2, QUARTER, FF), F32),
            pltpu.VMEM((FF, QUARTER), F32),
        ),
        in_specs=[any_, any_, vmem, vmem, vmem, any_, any_, any_, any_],
        out_specs=(vmem,) * 5,
        scratch_shapes=[
            pltpu.VMEM((256, D), BF16),
            pltpu.VMEM((ROWS, 256), BF16),
            pltpu.VMEM((ROWS, 128), F32),
            pltpu.VMEM(grid5, BF16),
            pltpu.VMEM(blocks, BF16),
            pltpu.VMEM(mid, BF16),
            pltpu.VMEM(mid_blocks, BF16),
            pltpu.VMEM(blocks, BF16),
            pltpu.VMEM((2, D, FF), BF16),
            pltpu.VMEM((FF, D), BF16),
            pltpu.VMEM((ROWS, FF), F32),
            pltpu.VMEM((ROWS, FF), F32),
            pltpu.VMEM((ROWS, FF), BF16),
            pltpu.VMEM((ROWS, FF), F32),
            pltpu.VMEM((2, ROWS, FF), BF16),
            pltpu.VMEM((3, 4, QUARTER, QUARTER), BF16),
            pltpu.VMEM((4, 3, QUARTER, QUARTER), BF16),
            pltpu.VMEM((4, 16, 128), F32),
            dma((6,)),
            dma((stages, 2)),
            dma((stages, 2)),
            dma((stages, 2)),
            dma((stages, 2)),
            dma((3,)),
            dma((5,)),
            dma((2,)),
            dma((1,)),
            dma((6,)),
            dma((1,)),
            dma((2,)),
        ],
        compiler_params=pltpu.CompilerParams(
            collective_id=0, has_side_effects=True, vmem_limit_bytes=53 << 20
        ),
        name="step",
    )(
        tokens[0], cotangent[0], slot_rows[0, 0], slot_count[0], slot_weight[0, 0],
        w_in[0], w_out[0], momentum_in[0], momentum_out[0],
    )
    outs = [pltpu.with_memory_space_constraint(o, pltpu.VMEM) for o in outs]
    outs = pl.pallas_call(
        write_out,
        out_shape=[pltpu.HBM(o.shape, o.dtype) for o in outs],
        in_specs=[vmem] * 5,
        out_specs=[pl.BlockSpec(memory_space=pltpu.HBM)] * 5,
        scratch_shapes=[dma((16,))],
        compiler_params=pltpu.CompilerParams(vmem_limit_bytes=1 << 20),
        name="write_out",
    )(*outs)
    outs = (outs[0], outs[1].reshape(2, D, FF)) + tuple(outs[2:])
    return tuple(o[None] for o in outs)


def solution(mesh):
    return jax.shard_map(
        shards,
        mesh=mesh,
        in_specs=(
            P("dp", "expert", None),
            P("dp", "expert", None),
            P("dp", "expert", None, None),
            P("dp", "expert", None),
            P("dp", "expert", None, None),
            P("expert", None, None, None),
            P("expert", None, None),
            P("expert", None, "dp", None),
            P("expert", None, "dp"),
        ),
        out_specs=(
            P("dp", "expert", None),
            P("expert", None, None, None),
            P("expert", None, None),
            P("expert", None, "dp", None),
            P("expert", None, "dp"),
        ),
        check_vma=False,
    )
```

```python
import jax
import jax.numpy as jnp
from jax import lax
from jax.experimental import pallas as pl
from jax.experimental.pallas import tpu as pltpu
from jax.sharding import PartitionSpec as P

EPS = 1e-06
MOMENTUM = 0.9
RATE = 0.1
MESH = pl.DeviceIdType.MESH

D = 2048
FF = 512
HALF = 1024
QUARTER = 512
CAP = 32
STAGES_X = 2
STAGES_G = 4
STAGES_R = 2
ROWS = 1024
BF16 = jnp.bfloat16
F32 = jnp.float32


def dot(a, b, ca, cb):
    return lax.dot_general(a, b, (((ca,), (cb,)), ((), ())), preferred_element_type=F32)


def kernel(
    tok_h, cot_h, rows_h, count_h, weight_h, win_h, wout_h, min_h, mout_h,
    tok, xs, nwout, mom_in, mom_out,
    cot, onehot, scale, send_x, send_g, mid_x, mid_g, gs_, win, wout,
    act_a, act_s, hid, dh, dgu, grad_s, grad_r, gram, rows_v, count_v, weight_v,
    load_sem, p1_send, p1_recv, p2_send, p2_recv,
    rs_send, rs_recv, gram_sem, ag_send, ag_recv, ag_last, fw_sem,
):
    z = lax.axis_index("dp")
    e = lax.axis_index("expert")
    x = e // 8
    y = lax.rem(e // 2, 4)
    c = lax.rem(e, 2)
    scale_in = D ** (-0.5)
    scale_out = FF ** (-0.5)

    def expert_id(px, py, pc):
        return (px * 4 + py) * 2 + pc

    barrier = pltpu.get_barrier_semaphore()

    def greet(device):
        pl.semaphore_signal(barrier, inc=1, device_id=device, device_id_type=MESH)

    for k in range(1, 8):
        greet((z, expert_id(lax.rem(x + k // 2, 4), y, lax.rem(c + k % 2, 2))))
    for k in range(2, 8):
        greet((z, expert_id(x, lax.rem(y + k // 2, 4), lax.rem(c + k % 2, 2))))
    for k in range(1, 4):
        greet((lax.rem(z + k, 4), e))

    loads = [
        (tok_h, tok), (cot_h, cot), (win_h, win), (wout_h, wout), (min_h, mom_in), (mout_h, mom_out),
        (rows_h, rows_v), (count_h, count_v), (weight_h, weight_v),
    ]
    load = [pltpu.make_async_copy(s, d, load_sem.at[i]) for i, (s, d) in enumerate(loads)]
    for copy in load[6:] + load[:2]:
        copy.start()

    for copy in load[6:]:
        copy.wait()

    rows_t = jnp.transpose(rows_v[...])
    weight_t = jnp.transpose(weight_v[...])
    valid = lax.broadcasted_iota(jnp.int32, (CAP, 32), 0) < count_v[...]
    scale_t = jnp.where(valid, weight_t, 0.0)
    lane = lax.broadcasted_iota(jnp.int32, (CAP, 256), 1)
    for k in range(32):
        onehot[k * CAP : (k + 1) * CAP, :] = (lane == rows_t[:, k : k + 1]).astype(F32).astype(BF16)
        scale[k * CAP : (k + 1) * CAP, :] = jnp.broadcast_to(scale_t[:, k : k + 1], (CAP, 128))

    def gather(src, dst, c0, w, scaled):
        def step(m, _):
            r0 = pl.multiple_of(m * 256, 256)
            hot = onehot[pl.ds(r0, 256), :]
            if scaled:
                for q in range(4):
                    v = dot(hot, src[:, q * QUARTER + c0 : q * QUARTER + c0 + w], 1, 0)
                    v = v * scale[pl.ds(r0, 256), 0:1]
                    dst[q, m, :, :, :, c0 : c0 + w] = v.astype(BF16).reshape(4, 2, CAP, w)
            else:
                for half in range(2):
                    col = half * HALF + c0
                    v = dot(hot, src[:, col : col + w], 1, 0)
                    dst[m, :, :, :, col : col + w] = v.astype(BF16).reshape(4, 2, CAP, w)
            return 0

        lax.fori_loop(0, 4, step, 0)

    def first_views(send, mid, c0, w, half, pa, pc):
        if send is send_g:
            col, both = pl.ds(c0, w), pl.ds(2 * half, 2)
            if half == 0:
                return send.at[both, pa, :, pc, :, col], mid.at[0, :, :, x, c, :, col]
            return send.at[both, :, pa, pc, :, col], mid.at[1, :, :, y, c, :, col]
        col, mcol = pl.ds(half * HALF + c0, w), pl.ds(c0, w)
        if half == 0:
            return send.at[pa, :, pc, :, col], mid.at[0, :, x, c, :, mcol]
        return send.at[:, pa, pc, :, col], mid.at[1, :, y, c, :, mcol]

    def second_views(mid, fin, c0, w, half, pa):
        if mid is mid_g:
            col, both = pl.ds(c0, w), pl.ds(2 * half, 2)
            src = mid.at[half, :, pa, :, :, :, col]
            if half == 0:
                return src, fin.at[both, :, y, :, :, col]
            return src, fin.at[both, x, :, :, :, col]
        src = mid.at[half, pa, :, :, :, pl.ds(c0, w)]
        if half == 0:
            return src, fin.at[c0 // QUARTER, :, y]
        return src, fin.at[2 + c0 // QUARTER, x]

    def p1_copy(send, mid, st, c0, w, half, k):
        pc = lax.rem(c + lax.rem(k, 2), 2)
        pa = lax.rem((x if half == 0 else y) + k // 2, 4)
        peer = expert_id(pa, y, pc) if half == 0 else expert_id(x, pa, pc)
        src, dst = first_views(send, mid, c0, w, half, pa, pc)
        return pltpu.make_async_remote_copy(
            src_ref=src, dst_ref=dst, send_sem=p1_send.at[st, half], recv_sem=p1_recv.at[st, half],
            device_id=(z, peer), device_id_type=MESH,
        )

    def p1_self(send, mid, st, c0, w, half):
        src, dst = first_views(send, mid, c0, w, half, x if half == 0 else y, c)
        return pltpu.make_async_copy(src, dst, p1_recv.at[st, half])

    def p2_copy(mid, fin, st, c0, w, half, k):
        pa = lax.rem((y if half == 0 else x) + k, 4)
        peer = expert_id(x, pa, c) if half == 0 else expert_id(pa, y, c)
        src, dst = second_views(mid, fin, c0, w, half, pa)
        return pltpu.make_async_remote_copy(
            src_ref=src, dst_ref=dst, send_sem=p2_send.at[st, half], recv_sem=p2_recv.at[st, half],
            device_id=(z, peer), device_id_type=MESH,
        )

    def p2_self(mid, fin, st, c0, w, half):
        src, dst = second_views(mid, fin, c0, w, half, y if half == 0 else x)
        return pltpu.make_async_copy(src, dst, p2_recv.at[st, half])

    def each(lo, hi, fn):
        def step(k, _):
            fn(k)
            return 0

        lax.fori_loop(lo, hi, step, 0)

    def settle(view, sem):
        pltpu.make_async_copy(view, view, sem).wait()

    def share(w, blocks):
        return hid.at[0 : blocks * 128, :] if w == QUARTER else onehot.at[0 : blocks * 128, :]

    def start_first(args):
        send, mid, fin, st, c0, w = args

        def go(k):
            p1_copy(send, mid, st, c0, w, 0, k).start()
            p1_copy(send, mid, st, c0, w, 1, k).start()

        each(1, 8, go)
        for half in range(2):
            p1_self(send, mid, st, c0, w, half).start()

    def forward(args):
        send, mid, fin, st, c0, w = args
        for half in range(2):
            landed = mid.at[half, :, :, :, :, :, pl.ds(c0, w)] if mid is mid_g else mid.at[half, :, :, :, :, pl.ds(c0, w)]
            settle(landed, p1_recv.at[st, half])
            settle(share(w, 7), p1_send.at[st, half])
            each(1, 4, lambda k: p2_copy(mid, fin, st, c0, w, half, k).start())
            p2_self(mid, fin, st, c0, w, half).start()

    def arrive(args):
        send, mid, fin, st, c0, w = args
        for half in range(2):
            if mid is mid_g:
                landed = fin.at[pl.ds(2 * half, 2), :, :, :, :, pl.ds(c0, w)]
            else:
                landed = fin.at[2 * half + c0 // QUARTER]
            settle(landed, p2_recv.at[st, half])
            settle(share(w, 6), p2_send.at[st, half])

    wx, wg, wr = HALF // STAGES_X, QUARTER // STAGES_G, HALF // STAGES_R
    ex = [(send_x, mid_x, xs, s, s * wx, wx) for s in range(STAGES_X)]
    eg = [(send_g, mid_g, gs_, STAGES_X + s, s * wg, wg) for s in range(STAGES_G)]
    er = [(send_x, mid_x, send_g, STAGES_X + STAGES_G + s, s * wr, wr) for s in range(STAGES_R)]

    def activate(m):
        rows = jnp.concatenate([xs[b, m].reshape(256, QUARTER) for b in range(4)], axis=1)
        r = pl.ds(pl.multiple_of(m * 256, 256), 256)
        gate = dot(rows, win[0], 1, 0) * scale_in
        up = dot(rows, win[1], 1, 0) * scale_in
        sig = jax.nn.sigmoid(gate)
        act = gate * sig
        hid[r, :] = (act * up).astype(BF16)
        act_a[r, :] = up * sig * (1.0 + gate * (1.0 - sig))
        act_s[r, :] = act

    def out_copy(s, q):
        src = grad_s.at[2, q, :, pl.ds(s * wg, wg)]
        dst = grad_r.at[z, 2, :, pl.ds(s * wg, wg)]
        return pltpu.make_async_remote_copy(
            src_ref=src, dst_ref=dst, send_sem=rs_send.at[2], recv_sem=rs_recv.at[4],
            device_id=(q, e), device_id_type=MESH,
        ), pltpu.make_async_copy(src, dst, rs_recv.at[4])

    def grad_out(s):
        cols = slice(s * wg, s * wg + wg)
        rows = jnp.concatenate([gs_[q, :, :, :, :, cols].reshape(ROWS, wg) for q in range(4)], axis=1)
        out = (dot(hid[...], rows, 0, 0) * scale_out).astype(BF16)
        for q in range(4):
            grad_s[2, q, :, cols] = out[:, q * wg : (q + 1) * wg]
            remote, local = out_copy(s, q)

            @pl.when(z != q)
            def _():
                remote.start()

            @pl.when(z == q)
            def _():
                local.start()

    def hidden_grad(s):
        def step(m, _):
            r = pl.ds(pl.multiple_of(m * 256, 256), 256)
            cols = slice(s * wg, s * wg + wg)
            rows = jnp.concatenate([gs_[q, m, :, :, :, cols].reshape(256, wg) for q in range(4)], axis=1)
            down = jnp.concatenate(
                [wout[:, q * QUARTER + s * wg : q * QUARTER + s * wg + wg] for q in range(4)], axis=1
            )
            acc = dot(rows, down, 1, 1)
            if s > 0:
                acc = acc + dh[r, :]
            if s < STAGES_G - 1:
                dh[r, :] = acc
            else:
                acc = acc * scale_out
                dgu[0, r, :] = (acc * act_a[r, :]).astype(BF16)
                dgu[1, r, :] = (acc * act_s[r, :]).astype(BF16)
            return 0

        lax.fori_loop(0, 4, step, 0)

    def in_copy(mat, hh, k):
        q = lax.rem(z + k, 4)
        part = pl.ds(hh * 256, 256)
        return pltpu.make_async_remote_copy(
            src_ref=grad_s.at[mat, q, part], dst_ref=grad_r.at[z, mat, part],
            send_sem=rs_send.at[mat], recv_sem=rs_recv.at[2 * mat + hh],
            device_id=(q, e), device_id_type=MESH,
        )

    def in_self(mat, hh):
        part = pl.ds(hh * 256, 256)
        return pltpu.make_async_copy(
            grad_s.at[mat, z, part], grad_r.at[z, mat, part], rs_recv.at[2 * mat + hh]
        )

    def grad_in(mat, hh):
        def step(j, _):
            k = lax.rem(1 + 2 * j + j // 2, 4)
            q = lax.rem(z + k, 4)
            rows = xs[q, :, :, :, :, hh * 256 : hh * 256 + 256].reshape(ROWS, 256)
            grad_s[mat, q, hh * 256 : hh * 256 + 256] = (dot(rows, dgu[mat], 0, 0) * scale_in).astype(BF16)

            @pl.when(k != 0)
            def _():
                in_copy(mat, hh, k).start()

            @pl.when(k == 0)
            def _():
                in_self(mat, hh).start()

            return 0

        lax.fori_loop(0, 4, step, 0)

    def rows_back(s):
        def step(m, _):
            r = pl.ds(pl.multiple_of(m * 256, 256), 256)
            for half in range(2):
                col = half * HALF + s * wr
                v = dot(dgu[0, r, :], win[0, col : col + wr, :], 1, 1)
                v = v + dot(dgu[1, r, :], win[1, col : col + wr, :], 1, 1)
                send_x[m, :, :, :, col : col + wr] = (v * scale_in).astype(BF16).reshape(4, 2, CAP, wr)
            return 0

        lax.fori_loop(0, 4, step, 0)

    pairs = [(0, 0), (1, 1), (2, 2), (3, 3), (0, 1), (0, 2), (0, 3), (1, 2), (1, 3), (2, 3)]

    def fold(v):
        total = None
        for i in range(v.shape[0] // 8):
            for j in range(v.shape[1] // 128):
                part = v[i * 8 : (i + 1) * 8, j * 128 : (j + 1) * 128]
                total = part if total is None else total + part
        return total

    def gram_of(mat, hh, sums):
        def step(i, sums):
            r = pl.ds(pl.multiple_of(hh * 256 + i * 16, 16), 16)
            g = [grad_r[s, mat, r, :].astype(F32) for s in range(4)]
            return tuple(t + fold(g[a] * g[b]) for t, (a, b) in zip(sums, pairs))

        return lax.fori_loop(0, 16, step, sums, unroll=2)

    load[0].wait()
    gather(tok, send_x, ex[0][4], wx, False)
    pl.semaphore_wait(barrier, 16)
    start_first(ex[0])
    for copy in load[2:6]:
        copy.start()
    gather(tok, send_x, ex[1][4], wx, False)
    start_first(ex[1])
    load[1].wait()
    gather(cot, send_g, eg[0][4], wg, True)
    gather(cot, send_g, eg[1][4], wg, True)
    forward(ex[0])
    start_first(eg[0])
    gather(cot, send_g, eg[2][4], wg, True)
    gather(cot, send_g, eg[3][4], wg, True)
    forward(ex[1])
    start_first(eg[1])
    forward(eg[0])
    start_first(eg[2])
    load[2].wait()
    load[3].wait()
    arrive(ex[0])
    arrive(ex[1])
    start_first(eg[3])
    each(0, 1, activate)
    forward(eg[1])
    each(1, 3, activate)
    forward(eg[2])
    each(3, 4, activate)
    arrive(eg[0])
    grad_out(0)
    forward(eg[3])
    hidden_grad(0)
    arrive(eg[1])
    grad_out(1)
    hidden_grad(1)
    arrive(eg[2])
    grad_out(2)
    hidden_grad(2)
    arrive(eg[3])
    grad_out(3)
    hidden_grad(3)
    for mat in range(2):
        for hh in range(2):
            grad_in(mat, hh)
    for s in range(STAGES_R):
        rows_back(s)
        start_first(er[s])

    sums = tuple(jnp.zeros((8, 128), F32) for _ in pairs)
    settle(grad_r.at[:, 2], rs_recv.at[4])
    settle(grad_s.at[2, 0:3], rs_send.at[2])
    sums = gram_of(2, 1, gram_of(2, 0, sums))
    for s in range(STAGES_R):
        forward(er[s])
    for mat in range(2):
        for hh in range(2):
            settle(grad_r.at[:, mat, pl.ds(hh * 256, 256)], rs_recv.at[2 * mat + hh])
            sums = gram_of(mat, hh, sums)
        settle(grad_s.at[mat, 0:3], rs_send.at[mat])

    own = jnp.concatenate([jnp.sum(t, axis=0, keepdims=True) for t in sums] + [jnp.zeros((6, 128), F32)], axis=0)
    gram[z] = own

    def gram_copy(k):
        return pltpu.make_async_remote_copy(
            src_ref=gram.at[z], dst_ref=gram.at[z], send_sem=gram_sem.at[0], recv_sem=gram_sem.at[1],
            device_id=(lax.rem(z + k, 4), e), device_id_type=MESH,
        )

    each(1, 4, lambda k: gram_copy(k).start())
    load[4].wait()
    load[5].wait()
    settle(gram.at[0:3], gram_sem.at[1])
    settle(gram.at[0:3], gram_sem.at[0])
    total = jnp.sum(gram[0] + gram[1] + gram[2] + gram[3], axis=1, keepdims=True)
    dots = {p: total[i : i + 1, :] for i, p in enumerate(pairs)}

    def coefficient(cross, norm):
        return 1.0 - cross / (2.0 * (norm + EPS))

    a0 = coefficient(dots[0, 2], dots[0, 0])
    a2 = coefficient(dots[0, 2], dots[2, 2])
    a1 = coefficient(dots[1, 3], dots[1, 1])
    a3 = coefficient(dots[1, 3], dots[3, 3])
    n0 = a0 * a0 * dots[0, 0] + 2.0 * a0 * a2 * dots[0, 2] + a2 * a2 * dots[2, 2]
    n1 = a1 * a1 * dots[1, 1] + 2.0 * a1 * a3 * dots[1, 3] + a3 * a3 * dots[3, 3]
    cross = a0 * (a1 * dots[0, 1] + a3 * dots[0, 3]) + a2 * (a1 * dots[1, 2] + a3 * dots[2, 3])
    b0 = coefficient(cross, jnp.maximum(n0, 0.0))
    b1 = coefficient(cross, jnp.maximum(n1, 0.0))
    coef = [b0 * a0, b1 * a1, b0 * a2, b1 * a3]

    def slot(mat, hh, owner):
        if mat < 2:
            return xs.at[2 * mat + owner // 2, 2 * lax.rem(owner, 2) + hh]
        return nwout.at[pl.ds(hh * 256, 256), pl.ds(pl.multiple_of(owner * QUARTER, QUARTER), QUARTER)]

    def ag_copy(mat, hh, direction):
        return pltpu.make_async_remote_copy(
            src_ref=slot(mat, hh, z), dst_ref=slot(mat, hh, z),
            send_sem=ag_send.at[0], recv_sem=ag_recv.at[2 * mat + hh] if direction == hh else ag_last.at[0],
            device_id=(lax.rem(z + (1 if direction == 0 else 3), 4), e), device_id_type=MESH,
        )

    def fw_copy(mat, hh):
        owner = lax.rem(z + (3 if hh == 0 else 1), 4)
        return pltpu.make_async_remote_copy(
            src_ref=slot(mat, hh, owner), dst_ref=slot(mat, hh, owner),
            send_sem=fw_sem.at[0], recv_sem=fw_sem.at[1],
            device_id=(lax.rem(z + (1 if hh == 0 else 3), 4), e), device_id_type=MESH,
        )

    for mat in range(3):
        for hh in range(2):

            def step(i, _):
                r = pl.multiple_of(hh * 256 + i * 32, 32)
                rr = pl.ds(r, 32)
                comb = coef[0] * grad_r[0, mat, rr, :].astype(F32)
                for s in range(1, 4):
                    comb = comb + coef[s] * grad_r[s, mat, rr, :].astype(F32)
                if mat < 2:
                    new = MOMENTUM * mom_in[mat, rr, :] + comb
                    mom_in[mat, rr, :] = new
                    old = win[mat, pl.ds(pl.multiple_of(z * QUARTER + r, 32), 32), :]
                else:
                    new = MOMENTUM * mom_out[rr, :] + comb
                    mom_out[rr, :] = new
                    old = wout[rr, pl.ds(pl.multiple_of(z * QUARTER, QUARTER), QUARTER)]
                value = (old.astype(F32) - RATE * new).astype(BF16)
                if mat < 2:
                    xs[2 * mat + z // 2, 2 * lax.rem(z, 2) + hh, i // 2, lax.rem(i, 2)] = value
                else:
                    nwout[rr, pl.ds(pl.multiple_of(z * QUARTER, QUARTER), QUARTER)] = value
                return 0

            lax.fori_loop(0, 8, step, 0)
            ag_copy(mat, hh, 0).start()
            ag_copy(mat, hh, 1).start()

    def pass_on(mat, hh):
        ag_copy(mat, hh, hh).wait_recv()
        fw_copy(mat, hh).start()

    for s in range(STAGES_R):
        arrive(er[s])

    def tokens_step(n, _):
        cols = pl.ds(pl.multiple_of(n * 512, 512), 512)
        rows = send_g[n].reshape(ROWS, 512)
        tok[:, cols] = dot(onehot[...], rows, 0, 0).astype(BF16)
        return 0

    lax.fori_loop(0, 4, tokens_step, 0)

    pass_on(0, 0)
    pass_on(0, 1)

    for mat in range(1, 3):
        for hh in range(2):
            pass_on(mat, hh)
    settle(grad_s.at[0, 0:3], ag_last.at[0])
    settle(grad_s.at[0:3, 0:2], ag_send.at[0])
    settle(grad_s.at[0, 0:3], fw_sem.at[0])
    settle(grad_s.at[0, 0:3], fw_sem.at[1])


def write_out(*refs):
    sources, targets, sem = refs[:5], refs[5:10], refs[10]
    copies = []
    for source, target in zip(sources, targets):
        parts = source.shape[0] if len(source.shape) != 2 else 2
        rows = source.shape[0] // parts
        for part in range(parts):
            at = pl.ds(part * rows, rows)
            copies.append(pltpu.make_async_copy(source.at[at], target.at[at], sem.at[len(copies)]))
    for copy in copies:
        copy.start()
    for copy in copies:
        copy.wait()


def shards(tokens, cotangent, slot_rows, slot_count, slot_weight, w_in, w_out, momentum_in, momentum_out):
    any_ = pl.BlockSpec(memory_space=pl.ANY)
    vmem = pl.BlockSpec(memory_space=pltpu.VMEM)
    stages = STAGES_X + STAGES_G + STAGES_R
    grid5 = (4, 4, 2, CAP, D)
    mid = (2, 4, 4, 2, CAP, HALF)
    blocks = (4, 4, 4, 2, CAP, QUARTER)
    mid_blocks = (2, 2, 4, 4, 2, CAP, QUARTER)
    dma = pltpu.SemaphoreType.DMA
    outs = pl.pallas_call(
        kernel,
        out_shape=(
            pltpu.VMEM((256, D), BF16),
            pltpu.VMEM(blocks, BF16),
            pltpu.VMEM((FF, D), BF16),
            pltpu.VMEM((2, QUARTER, FF), F32),
            pltpu.VMEM((FF, QUARTER), F32),
        ),
        in_specs=[any_] * 9,
        out_specs=(vmem,) * 5,
        scratch_shapes=[
            pltpu.VMEM((256, D), BF16),
            pltpu.VMEM((ROWS, 256), BF16),
            pltpu.VMEM((ROWS, 128), F32),
            pltpu.VMEM(grid5, BF16),
            pltpu.VMEM(blocks, BF16),
            pltpu.VMEM(mid, BF16),
            pltpu.VMEM(mid_blocks, BF16),
            pltpu.VMEM(blocks, BF16),
            pltpu.VMEM((2, D, FF), BF16),
            pltpu.VMEM((FF, D), BF16),
            pltpu.VMEM((ROWS, FF), F32),
            pltpu.VMEM((ROWS, FF), F32),
            pltpu.VMEM((ROWS, FF), BF16),
            pltpu.VMEM((ROWS, FF), F32),
            pltpu.VMEM((2, ROWS, FF), BF16),
            pltpu.VMEM((3, 4, QUARTER, QUARTER), BF16),
            pltpu.VMEM((4, 3, QUARTER, QUARTER), BF16),
            pltpu.VMEM((4, 16, 128), F32),
            pltpu.VMEM((32, CAP), jnp.int32),
            pltpu.VMEM((1, 32), jnp.int32),
            pltpu.VMEM((32, CAP), F32),
            dma((9,)),
            dma((stages, 2)),
            dma((stages, 2)),
            dma((stages, 2)),
            dma((stages, 2)),
            dma((3,)),
            dma((5,)),
            dma((2,)),
            dma((1,)),
            dma((6,)),
            dma((1,)),
            dma((2,)),
        ],
        compiler_params=pltpu.CompilerParams(
            collective_id=0, has_side_effects=True, vmem_limit_bytes=53 << 20
        ),
        name="step",
    )(
        tokens[0], cotangent[0], slot_rows[0, 0], slot_count[0], slot_weight[0, 0],
        w_in[0], w_out[0], momentum_in[0], momentum_out[0],
    )
    outs = [pltpu.with_memory_space_constraint(o, pltpu.VMEM) for o in outs]
    outs = pl.pallas_call(
        write_out,
        out_shape=[pltpu.HBM(o.shape, o.dtype) for o in outs],
        in_specs=[vmem] * 5,
        out_specs=[pl.BlockSpec(memory_space=pltpu.HBM)] * 5,
        scratch_shapes=[dma((16,))],
        compiler_params=pltpu.CompilerParams(vmem_limit_bytes=1 << 20),
        name="write_out",
    )(*outs)
    outs = (outs[0], outs[1].reshape(2, D, FF)) + tuple(outs[2:])
    return tuple(o[None] for o in outs)


def solution(mesh):
    return jax.shard_map(
        shards,
        mesh=mesh,
        in_specs=(
            P("dp", "expert", None),
            P("dp", "expert", None),
            P("dp", "expert", None, None),
            P("dp", "expert", None),
            P("dp", "expert", None, None),
            P("expert", None, None, None),
            P("expert", None, None),
            P("expert", None, "dp", None),
            P("expert", None, "dp"),
        ),
        out_specs=(
            P("dp", "expert", None),
            P("expert", None, None, None),
            P("expert", None, None),
            P("expert", None, "dp", None),
            P("expert", None, "dp"),
        ),
        check_vma=False,
    )
```

```python
import jax
import jax.numpy as jnp
from jax import lax
from jax.experimental import pallas as pl
from jax.experimental.pallas import tpu as pltpu
from jax.sharding import PartitionSpec as P

EPS = 1e-06
MOMENTUM = 0.9
RATE = 0.1
MESH = pl.DeviceIdType.MESH

D = 2048
FF = 512
HALF = 1024
QUARTER = 512
CAP = 32
STAGES_X = 2
STAGES_G = 4
STAGES_R = 2
ROWS = 1024
BF16 = jnp.bfloat16
F32 = jnp.float32


def dot(a, b, ca, cb):
    return lax.dot_general(a, b, (((ca,), (cb,)), ((), ())), preferred_element_type=F32)


def kernel(
    tok_h, cot_h, rows_h, count_h, weight_h, win_h, wout_h, min_h, mout_h,
    tok, xs, nwout, mom_in, mom_out,
    cot, onehot, scale, send_x, send_g, mid_x, mid_g, gs_, win, wout,
    act_a, act_s, hid, dh, dgu, grad_s, grad_r, gram, rows_v, count_v, weight_v,
    load_sem, p1_send, p1_recv, p2_send, p2_recv,
    rs_send, rs_recv, gram_sem, ag_send, ag_recv, ag_last, fw_sem,
):
    z = lax.axis_index("dp")
    e = lax.axis_index("expert")
    x = e // 8
    y = lax.rem(e // 2, 4)
    c = lax.rem(e, 2)
    scale_in = D ** (-0.5)
    scale_out = FF ** (-0.5)

    def expert_id(px, py, pc):
        return (px * 4 + py) * 2 + pc

    barrier = pltpu.get_barrier_semaphore()

    def greet(device):
        pl.semaphore_signal(barrier, inc=1, device_id=device, device_id_type=MESH)

    for k in range(1, 8):
        greet((z, expert_id(lax.rem(x + k // 2, 4), y, lax.rem(c + k % 2, 2))))
    for k in range(2, 8):
        greet((z, expert_id(x, lax.rem(y + k // 2, 4), lax.rem(c + k % 2, 2))))
    for k in range(1, 4):
        greet((lax.rem(z + k, 4), e))

    loads = [
        (tok_h, tok), (cot_h, cot), (win_h, win), (wout_h, wout), (min_h, mom_in), (mout_h, mom_out),
        (rows_h, rows_v), (count_h, count_v), (weight_h, weight_v),
    ]
    load = [pltpu.make_async_copy(s, d, load_sem.at[i]) for i, (s, d) in enumerate(loads)]
    for copy in load[6:] + load[:2]:
        copy.start()

    for copy in load[6:]:
        copy.wait()

    rows_t = jnp.transpose(rows_v[...])
    weight_t = jnp.transpose(weight_v[...])
    valid = lax.broadcasted_iota(jnp.int32, (CAP, 32), 0) < count_v[...]
    scale_t = jnp.where(valid, weight_t, 0.0)
    lane = lax.broadcasted_iota(jnp.int32, (CAP, 256), 1)
    for k in range(32):
        onehot[k * CAP : (k + 1) * CAP, :] = (lane == rows_t[:, k : k + 1]).astype(F32).astype(BF16)
        scale[k * CAP : (k + 1) * CAP, :] = jnp.broadcast_to(scale_t[:, k : k + 1], (CAP, 128))

    def gather(src, dst, c0, w, scaled):
        def step(m, _):
            r0 = pl.multiple_of(m * 256, 256)
            hot = onehot[pl.ds(r0, 256), :]
            if scaled:
                for q in range(4):
                    v = dot(hot, src[:, q * QUARTER + c0 : q * QUARTER + c0 + w], 1, 0)
                    v = v * scale[pl.ds(r0, 256), 0:1]
                    dst[q, m, :, :, :, c0 : c0 + w] = v.astype(BF16).reshape(4, 2, CAP, w)
            else:
                for half in range(2):
                    col = half * HALF + c0
                    v = dot(hot, src[:, col : col + w], 1, 0)
                    dst[m, :, :, :, col : col + w] = v.astype(BF16).reshape(4, 2, CAP, w)
            return 0

        lax.fori_loop(0, 4, step, 0)

    def first_views(send, mid, c0, w, half, pa, pc):
        if send is send_g:
            col, both = pl.ds(c0, w), pl.ds(2 * half, 2)
            if half == 0:
                return send.at[both, pa, :, pc, :, col], mid.at[0, :, :, x, c, :, col]
            return send.at[both, :, pa, pc, :, col], mid.at[1, :, :, y, c, :, col]
        col, mcol = pl.ds(half * HALF + c0, w), pl.ds(c0, w)
        if half == 0:
            return send.at[pa, :, pc, :, col], mid.at[0, :, x, c, :, mcol]
        return send.at[:, pa, pc, :, col], mid.at[1, :, y, c, :, mcol]

    def second_views(mid, fin, c0, w, half, pa):
        if mid is mid_g:
            col, both = pl.ds(c0, w), pl.ds(2 * half, 2)
            src = mid.at[half, :, pa, :, :, :, col]
            if half == 0:
                return src, fin.at[both, :, y, :, :, col]
            return src, fin.at[both, x, :, :, :, col]
        src = mid.at[half, pa, :, :, :, pl.ds(c0, w)]
        if half == 0:
            return src, fin.at[c0 // QUARTER, :, y]
        return src, fin.at[2 + c0 // QUARTER, x]

    def p1_copy(send, mid, st, c0, w, half, k):
        pc = lax.rem(c + lax.rem(k, 2), 2)
        pa = lax.rem((x if half == 0 else y) + k // 2, 4)
        peer = expert_id(pa, y, pc) if half == 0 else expert_id(x, pa, pc)
        src, dst = first_views(send, mid, c0, w, half, pa, pc)
        return pltpu.make_async_remote_copy(
            src_ref=src, dst_ref=dst, send_sem=p1_send.at[st, half], recv_sem=p1_recv.at[st, half],
            device_id=(z, peer), device_id_type=MESH,
        )

    def p1_self(send, mid, st, c0, w, half):
        src, dst = first_views(send, mid, c0, w, half, x if half == 0 else y, c)
        return pltpu.make_async_copy(src, dst, p1_recv.at[st, half])

    def p2_copy(mid, fin, st, c0, w, half, k):
        pa = lax.rem((y if half == 0 else x) + k, 4)
        peer = expert_id(x, pa, c) if half == 0 else expert_id(pa, y, c)
        src, dst = second_views(mid, fin, c0, w, half, pa)
        return pltpu.make_async_remote_copy(
            src_ref=src, dst_ref=dst, send_sem=p2_send.at[st, half], recv_sem=p2_recv.at[st, half],
            device_id=(z, peer), device_id_type=MESH,
        )

    def p2_self(mid, fin, st, c0, w, half):
        src, dst = second_views(mid, fin, c0, w, half, y if half == 0 else x)
        return pltpu.make_async_copy(src, dst, p2_recv.at[st, half])

    def each(lo, hi, fn):
        def step(k, _):
            fn(k)
            return 0

        lax.fori_loop(lo, hi, step, 0)

    def settle(view, sem):
        pltpu.make_async_copy(view, view, sem).wait()

    def share(w, blocks):
        return hid.at[0 : blocks * 128, :] if w == QUARTER else onehot.at[0 : blocks * 128, :]

    def start_first(args):
        send, mid, fin, st, c0, w = args

        def go(k):
            p1_copy(send, mid, st, c0, w, 0, k).start()
            p1_copy(send, mid, st, c0, w, 1, k).start()

        each(1, 8, go)
        for half in range(2):
            p1_self(send, mid, st, c0, w, half).start()

    def forward(args):
        send, mid, fin, st, c0, w = args
        for half in range(2):
            landed = mid.at[half, :, :, :, :, :, pl.ds(c0, w)] if mid is mid_g else mid.at[half, :, :, :, :, pl.ds(c0, w)]
            settle(landed, p1_recv.at[st, half])
            settle(share(w, 7), p1_send.at[st, half])
            each(1, 4, lambda k: p2_copy(mid, fin, st, c0, w, half, k).start())
            p2_self(mid, fin, st, c0, w, half).start()

    def arrive(args):
        send, mid, fin, st, c0, w = args
        for half in range(2):
            if mid is mid_g:
                landed = fin.at[pl.ds(2 * half, 2), :, :, :, :, pl.ds(c0, w)]
            else:
                landed = fin.at[2 * half + c0 // QUARTER]
            settle(landed, p2_recv.at[st, half])
            settle(share(w, 6), p2_send.at[st, half])

    wx, wg, wr = HALF // STAGES_X, QUARTER // STAGES_G, HALF // STAGES_R
    ex = [(send_x, mid_x, xs, s, s * wx, wx) for s in range(STAGES_X)]
    eg = [(send_g, mid_g, gs_, STAGES_X + s, s * wg, wg) for s in range(STAGES_G)]
    er = [(send_x, mid_x, send_g, STAGES_X + STAGES_G + s, s * wr, wr) for s in range(STAGES_R)]

    def activate(m):
        rows = jnp.concatenate([xs[b, m].reshape(256, QUARTER) for b in range(4)], axis=1)
        r = pl.ds(pl.multiple_of(m * 256, 256), 256)
        gate = dot(rows, win[0], 1, 0) * scale_in
        up = dot(rows, win[1], 1, 0) * scale_in
        sig = jax.nn.sigmoid(gate)
        act = gate * sig
        hid[r, :] = (act * up).astype(BF16)
        act_a[r, :] = up * sig * (1.0 + gate * (1.0 - sig))
        act_s[r, :] = act

    def out_copy(s, q):
        src = grad_s.at[2, q, :, pl.ds(s * wg, wg)]
        dst = grad_r.at[z, 2, :, pl.ds(s * wg, wg)]
        return pltpu.make_async_remote_copy(
            src_ref=src, dst_ref=dst, send_sem=rs_send.at[2], recv_sem=rs_recv.at[4],
            device_id=(q, e), device_id_type=MESH,
        ), pltpu.make_async_copy(src, dst, rs_recv.at[4])

    def grad_out(s):
        cols = slice(s * wg, s * wg + wg)
        rows = jnp.concatenate([gs_[q, :, :, :, :, cols].reshape(ROWS, wg) for q in range(4)], axis=1)
        out = (dot(hid[...], rows, 0, 0) * scale_out).astype(BF16)
        for q in range(4):
            grad_s[2, q, :, cols] = out[:, q * wg : (q + 1) * wg]
            remote, local = out_copy(s, q)

            @pl.when(z != q)
            def _():
                remote.start()

            @pl.when(z == q)
            def _():
                local.start()

    def hidden_grad(s):
        def step(m, _):
            r = pl.ds(pl.multiple_of(m * 256, 256), 256)
            cols = slice(s * wg, s * wg + wg)
            rows = jnp.concatenate([gs_[q, m, :, :, :, cols].reshape(256, wg) for q in range(4)], axis=1)
            down = jnp.concatenate(
                [wout[:, q * QUARTER + s * wg : q * QUARTER + s * wg + wg] for q in range(4)], axis=1
            )
            acc = dot(rows, down, 1, 1)
            if s > 0:
                acc = acc + dh[r, :]
            if s < STAGES_G - 1:
                dh[r, :] = acc
            else:
                acc = acc * scale_out
                dgu[0, r, :] = (acc * act_a[r, :]).astype(BF16)
                dgu[1, r, :] = (acc * act_s[r, :]).astype(BF16)
            return 0

        lax.fori_loop(0, 4, step, 0)

    def in_copy(mat, hh, k):
        q = lax.rem(z + k, 4)
        part = pl.ds(hh * 256, 256)
        return pltpu.make_async_remote_copy(
            src_ref=grad_s.at[mat, q, part], dst_ref=grad_r.at[z, mat, part],
            send_sem=rs_send.at[mat], recv_sem=rs_recv.at[2 * mat + hh],
            device_id=(q, e), device_id_type=MESH,
        )

    def in_self(mat, hh):
        part = pl.ds(hh * 256, 256)
        return pltpu.make_async_copy(
            grad_s.at[mat, z, part], grad_r.at[z, mat, part], rs_recv.at[2 * mat + hh]
        )

    def grad_in(mat, hh):
        def step(j, _):
            k = lax.rem(1 + 2 * j + j // 2, 4)
            q = lax.rem(z + k, 4)
            rows = xs[q, :, :, :, :, hh * 256 : hh * 256 + 256].reshape(ROWS, 256)
            grad_s[mat, q, hh * 256 : hh * 256 + 256] = (dot(rows, dgu[mat], 0, 0) * scale_in).astype(BF16)

            @pl.when(k != 0)
            def _():
                in_copy(mat, hh, k).start()

            @pl.when(k == 0)
            def _():
                in_self(mat, hh).start()

            return 0

        lax.fori_loop(0, 4, step, 0)

    def rows_back(s):
        def step(m, _):
            r = pl.ds(pl.multiple_of(m * 256, 256), 256)
            for half in range(2):
                col = half * HALF + s * wr
                v = dot(dgu[0, r, :], win[0, col : col + wr, :], 1, 1)
                v = v + dot(dgu[1, r, :], win[1, col : col + wr, :], 1, 1)
                send_x[m, :, :, :, col : col + wr] = (v * scale_in).astype(BF16).reshape(4, 2, CAP, wr)
            return 0

        lax.fori_loop(0, 4, step, 0)

    pairs = [(0, 0), (1, 1), (2, 2), (3, 3), (0, 1), (0, 2), (0, 3), (1, 2), (1, 3), (2, 3)]

    def fold(v):
        total = None
        for i in range(v.shape[0] // 8):
            for j in range(v.shape[1] // 128):
                part = v[i * 8 : (i + 1) * 8, j * 128 : (j + 1) * 128]
                total = part if total is None else total + part
        return total

    def gram_of(mat, hh, sums):
        def step(i, sums):
            r = pl.ds(pl.multiple_of(hh * 256 + i * 16, 16), 16)
            g = [grad_r[s, mat, r, :].astype(F32) for s in range(4)]
            return tuple(t + fold(g[a] * g[b]) for t, (a, b) in zip(sums, pairs))

        return lax.fori_loop(0, 16, step, sums, unroll=2)

    load[0].wait()
    gather(tok, send_x, ex[0][4], wx, False)
    pl.semaphore_wait(barrier, 16)
    start_first(ex[0])
    for copy in load[2:6]:
        copy.start()
    gather(tok, send_x, ex[1][4], wx, False)
    start_first(ex[1])
    load[1].wait()
    gather(cot, send_g, eg[0][4], wg, True)
    gather(cot, send_g, eg[1][4], wg, True)
    forward(ex[0])
    start_first(eg[0])
    gather(cot, send_g, eg[2][4], wg, True)
    gather(cot, send_g, eg[3][4], wg, True)
    forward(ex[1])
    start_first(eg[1])
    forward(eg[0])
    start_first(eg[2])
    load[2].wait()
    load[3].wait()
    arrive(ex[0])
    arrive(ex[1])
    start_first(eg[3])
    each(0, 2, activate)
    forward(eg[1])
    each(2, 4, activate)
    forward(eg[2])
    arrive(eg[0])
    grad_out(0)
    forward(eg[3])
    hidden_grad(0)
    arrive(eg[1])
    grad_out(1)
    hidden_grad(1)
    arrive(eg[2])
    grad_out(2)
    hidden_grad(2)
    arrive(eg[3])
    grad_out(3)
    hidden_grad(3)
    for mat in range(2):
        for hh in range(2):
            grad_in(mat, hh)
    for s in range(STAGES_R):
        rows_back(s)
        start_first(er[s])

    sums = tuple(jnp.zeros((8, 128), F32) for _ in pairs)
    settle(grad_r.at[:, 2], rs_recv.at[4])
    settle(grad_s.at[2, 0:3], rs_send.at[2])
    sums = gram_of(2, 1, gram_of(2, 0, sums))
    for s in range(STAGES_R):
        forward(er[s])
    for mat in range(2):
        for hh in range(2):
            settle(grad_r.at[:, mat, pl.ds(hh * 256, 256)], rs_recv.at[2 * mat + hh])
            sums = gram_of(mat, hh, sums)
        settle(grad_s.at[mat, 0:3], rs_send.at[mat])

    own = jnp.concatenate([jnp.sum(t, axis=0, keepdims=True) for t in sums] + [jnp.zeros((6, 128), F32)], axis=0)
    gram[z] = own

    def gram_copy(k):
        return pltpu.make_async_remote_copy(
            src_ref=gram.at[z], dst_ref=gram.at[z], send_sem=gram_sem.at[0], recv_sem=gram_sem.at[1],
            device_id=(lax.rem(z + k, 4), e), device_id_type=MESH,
        )

    each(1, 4, lambda k: gram_copy(k).start())
    load[4].wait()
    load[5].wait()
    settle(gram.at[0:3], gram_sem.at[1])
    settle(gram.at[0:3], gram_sem.at[0])
    total = jnp.sum(gram[0] + gram[1] + gram[2] + gram[3], axis=1, keepdims=True)
    dots = {p: total[i : i + 1, :] for i, p in enumerate(pairs)}

    def coefficient(cross, norm):
        return 1.0 - cross / (2.0 * (norm + EPS))

    a0 = coefficient(dots[0, 2], dots[0, 0])
    a2 = coefficient(dots[0, 2], dots[2, 2])
    a1 = coefficient(dots[1, 3], dots[1, 1])
    a3 = coefficient(dots[1, 3], dots[3, 3])
    n0 = a0 * a0 * dots[0, 0] + 2.0 * a0 * a2 * dots[0, 2] + a2 * a2 * dots[2, 2]
    n1 = a1 * a1 * dots[1, 1] + 2.0 * a1 * a3 * dots[1, 3] + a3 * a3 * dots[3, 3]
    cross = a0 * (a1 * dots[0, 1] + a3 * dots[0, 3]) + a2 * (a1 * dots[1, 2] + a3 * dots[2, 3])
    b0 = coefficient(cross, jnp.maximum(n0, 0.0))
    b1 = coefficient(cross, jnp.maximum(n1, 0.0))
    coef = [b0 * a0, b1 * a1, b0 * a2, b1 * a3]

    def slot(mat, hh, owner):
        if mat < 2:
            return xs.at[2 * mat + owner // 2, 2 * lax.rem(owner, 2) + hh]
        return nwout.at[pl.ds(hh * 256, 256), pl.ds(pl.multiple_of(owner * QUARTER, QUARTER), QUARTER)]

    def ag_copy(mat, hh, direction):
        return pltpu.make_async_remote_copy(
            src_ref=slot(mat, hh, z), dst_ref=slot(mat, hh, z),
            send_sem=ag_send.at[0], recv_sem=ag_recv.at[2 * mat + hh] if direction == hh else ag_last.at[0],
            device_id=(lax.rem(z + (1 if direction == 0 else 3), 4), e), device_id_type=MESH,
        )

    def fw_copy(mat, hh):
        owner = lax.rem(z + (3 if hh == 0 else 1), 4)
        return pltpu.make_async_remote_copy(
            src_ref=slot(mat, hh, owner), dst_ref=slot(mat, hh, owner),
            send_sem=fw_sem.at[0], recv_sem=fw_sem.at[1],
            device_id=(lax.rem(z + (1 if hh == 0 else 3), 4), e), device_id_type=MESH,
        )

    for mat in range(3):
        for hh in range(2):

            def step(i, _):
                r = pl.multiple_of(hh * 256 + i * 32, 32)
                rr = pl.ds(r, 32)
                comb = coef[0] * grad_r[0, mat, rr, :].astype(F32)
                for s in range(1, 4):
                    comb = comb + coef[s] * grad_r[s, mat, rr, :].astype(F32)
                if mat < 2:
                    new = MOMENTUM * mom_in[mat, rr, :] + comb
                    mom_in[mat, rr, :] = new
                    old = win[mat, pl.ds(pl.multiple_of(z * QUARTER + r, 32), 32), :]
                else:
                    new = MOMENTUM * mom_out[rr, :] + comb
                    mom_out[rr, :] = new
                    old = wout[rr, pl.ds(pl.multiple_of(z * QUARTER, QUARTER), QUARTER)]
                value = (old.astype(F32) - RATE * new).astype(BF16)
                if mat < 2:
                    xs[2 * mat + z // 2, 2 * lax.rem(z, 2) + hh, i // 2, lax.rem(i, 2)] = value
                else:
                    nwout[rr, pl.ds(pl.multiple_of(z * QUARTER, QUARTER), QUARTER)] = value
                return 0

            lax.fori_loop(0, 8, step, 0)
            ag_copy(mat, hh, 0).start()
            ag_copy(mat, hh, 1).start()

    def pass_on(mat, hh):
        ag_copy(mat, hh, hh).wait_recv()
        fw_copy(mat, hh).start()

    for s in range(STAGES_R):
        arrive(er[s])

    def tokens_step(n, _):
        cols = pl.ds(pl.multiple_of(n * 512, 512), 512)
        rows = send_g[n].reshape(ROWS, 512)
        tok[:, cols] = dot(onehot[...], rows, 0, 0).astype(BF16)
        return 0

    lax.fori_loop(0, 4, tokens_step, 0)

    pass_on(0, 0)
    pass_on(0, 1)

    for mat in range(1, 3):
        for hh in range(2):
            pass_on(mat, hh)
    settle(grad_s.at[0, 0:3], ag_last.at[0])
    settle(grad_s.at[0:3, 0:2], ag_send.at[0])
    settle(grad_s.at[0, 0:3], fw_sem.at[0])
    settle(grad_s.at[0, 0:3], fw_sem.at[1])


def write_out(*refs):
    sources, targets, sem = refs[:5], refs[5:10], refs[10]
    copies = []
    for source, target in zip(sources, targets):
        parts = source.shape[0] if len(source.shape) != 2 else 2
        rows = source.shape[0] // parts
        for part in range(parts):
            at = pl.ds(part * rows, rows)
            copies.append(pltpu.make_async_copy(source.at[at], target.at[at], sem.at[len(copies)]))
    for copy in copies:
        copy.start()
    for copy in copies:
        copy.wait()


def shards(tokens, cotangent, slot_rows, slot_count, slot_weight, w_in, w_out, momentum_in, momentum_out):
    any_ = pl.BlockSpec(memory_space=pl.ANY)
    vmem = pl.BlockSpec(memory_space=pltpu.VMEM)
    stages = STAGES_X + STAGES_G + STAGES_R
    grid5 = (4, 4, 2, CAP, D)
    mid = (2, 4, 4, 2, CAP, HALF)
    blocks = (4, 4, 4, 2, CAP, QUARTER)
    mid_blocks = (2, 2, 4, 4, 2, CAP, QUARTER)
    dma = pltpu.SemaphoreType.DMA
    outs = pl.pallas_call(
        kernel,
        out_shape=(
            pltpu.VMEM((256, D), BF16),
            pltpu.VMEM(blocks, BF16),
            pltpu.VMEM((FF, D), BF16),
            pltpu.VMEM((2, QUARTER, FF), F32),
            pltpu.VMEM((FF, QUARTER), F32),
        ),
        in_specs=[any_] * 9,
        out_specs=(vmem,) * 5,
        scratch_shapes=[
            pltpu.VMEM((256, D), BF16),
            pltpu.VMEM((ROWS, 256), BF16),
            pltpu.VMEM((ROWS, 128), F32),
            pltpu.VMEM(grid5, BF16),
            pltpu.VMEM(blocks, BF16),
            pltpu.VMEM(mid, BF16),
            pltpu.VMEM(mid_blocks, BF16),
            pltpu.VMEM(blocks, BF16),
            pltpu.VMEM((2, D, FF), BF16),
            pltpu.VMEM((FF, D), BF16),
            pltpu.VMEM((ROWS, FF), F32),
            pltpu.VMEM((ROWS, FF), F32),
            pltpu.VMEM((ROWS, FF), BF16),
            pltpu.VMEM((ROWS, FF), F32),
            pltpu.VMEM((2, ROWS, FF), BF16),
            pltpu.VMEM((3, 4, QUARTER, QUARTER), BF16),
            pltpu.VMEM((4, 3, QUARTER, QUARTER), BF16),
            pltpu.VMEM((4, 16, 128), F32),
            pltpu.VMEM((32, CAP), jnp.int32),
            pltpu.VMEM((1, 32), jnp.int32),
            pltpu.VMEM((32, CAP), F32),
            dma((9,)),
            dma((stages, 2)),
            dma((stages, 2)),
            dma((stages, 2)),
            dma((stages, 2)),
            dma((3,)),
            dma((5,)),
            dma((2,)),
            dma((1,)),
            dma((6,)),
            dma((1,)),
            dma((2,)),
        ],
        compiler_params=pltpu.CompilerParams(
            collective_id=0, has_side_effects=True, vmem_limit_bytes=53 << 20
        ),
        name="step",
    )(
        tokens[0], cotangent[0], slot_rows[0, 0], slot_count[0], slot_weight[0, 0],
        w_in[0], w_out[0], momentum_in[0], momentum_out[0],
    )
    outs = [pltpu.with_memory_space_constraint(o, pltpu.VMEM) for o in outs]
    outs = pl.pallas_call(
        write_out,
        out_shape=[pltpu.HBM(o.shape, o.dtype) for o in outs],
        in_specs=[vmem] * 5,
        out_specs=[pl.BlockSpec(memory_space=pltpu.HBM)] * 5,
        scratch_shapes=[dma((16,))],
        compiler_params=pltpu.CompilerParams(vmem_limit_bytes=1 << 20),
        name="write_out",
    )(*outs)
    outs = (outs[0], outs[1].reshape(2, D, FF)) + tuple(outs[2:])
    return tuple(o[None] for o in outs)


def solution(mesh):
    return jax.shard_map(
        shards,
        mesh=mesh,
        in_specs=(
            P("dp", "expert", None),
            P("dp", "expert", None),
            P("dp", "expert", None, None),
            P("dp", "expert", None),
            P("dp", "expert", None, None),
            P("expert", None, None, None),
            P("expert", None, None),
            P("expert", None, "dp", None),
            P("expert", None, "dp"),
        ),
        out_specs=(
            P("dp", "expert", None),
            P("expert", None, None, None),
            P("expert", None, None),
            P("expert", None, "dp", None),
            P("expert", None, "dp"),
        ),
        check_vma=False,
    )
```
